32 devices in a mesh: doc: 8 (over y, x, core), head: 4 (over z).
Axes of the slice: x: 2, y: 2, z: 4, core: 2. Of those that a mesh axis runs over, the one named last changes fastest.
Arguments:
- queries: bfloat16 [2048, 2048], P(('doc', 'head')), may hold values from -6 to 6
- keys: bfloat16 [2048, 2048], P(('doc', 'head')), may hold values from -6 to 6
- values: bfloat16 [2048, 2048], P(('doc', 'head')), may hold values from -6 to 6
- log_decay: bfloat16 [2048, 2048], P(('doc', 'head')), may hold values from -1 to 0
- beta_logit: bfloat16 [2048, 16], P(('doc', 'head')), may hold values from -6 to 6
- block_owner: int32 [8, 16], replicated, may hold values from 0 to 7, as said below
- block_start: int32 [8, 16], replicated, may hold values from 0 to 1, as said below
- gain: float32 [2048], P('head'), may hold values from 0.25 to 1.75
Outputs:
- attended: bfloat16 [4096, 2048], P('doc', 'head')
The draws below stay inside these ranges and needn't reach their ends.
Inputs may be any that keep to these rules, and one draw needn't show every extreme that they name: `block_owner`: every block of index d of doc goes to owner (d + k) mod 8 for some k from 0 to 3; the blocks of one index with one owner form one run; a document lies in one run; at most 8 blocks of one index go to one owner, and exactly 8 to some owner of every index. `block_start`: the first block of every run of block_owner is 1; a document has 1 to 8 blocks.
All inputs are finite; a program needn't handle non-finite values.
Results may differ from the reference program's by a relative error of at most 0.001.
Values may be sent and summed in bfloat16 or wider, within the bound.
A program may use at most 64 MiB of HBM per device.

```python
import math
import jax
import jax.numpy as jnp
from jax import lax

PER_QUERY_WIDTH = 128
OWNED_PARTITION = 16
ALL_WIDTH_SUM = 2048
TOK_DEV = 64
BLOCK = 16
TILE = 128
RUNS = 4
ROWTOK = 256
RB = 16
CAP = 8
OS = 512
SEQUENCE_LENGTH = 2048
N_DOC = 8


def block_lists(floor_value):
    mean = RB // RUNS

    def one_row(row_key, row_index):
        parts_keys = jax.random.split(row_key, 5)
        order = jax.random.permutation(parts_keys[0], RUNS)
        delta = jax.random.randint(parts_keys[1], (RUNS // 2,), -mean, mean + 1)
        forced = jax.random.randint(parts_keys[2], (), 0, RUNS // 2)
        delta = jnp.where(jnp.arange(RUNS // 2) == forced, mean, delta)
        lengths = jnp.stack([mean + delta, mean - delta], axis=1).reshape(RUNS)
        ends = jnp.cumsum(lengths)
        begins = ends - lengths
        blocks = jnp.arange(RB)
        which = jnp.sum((blocks[:, None] >= ends[None, :]).astype(jnp.int32), axis=1)
        owner = jnp.mod(row_index + order[which], N_DOC)
        place = blocks - begins[which]
        cutting = jax.random.randint(parts_keys[3], (RUNS,), 1, max(2 * mean, 2))
        splits = jax.random.randint(parts_keys[4], (RUNS,), 0, 2)
        starts = (place == 0) | (splits[which] == 1) & (place == cutting[which])
        return (owner.astype(jnp.int32), starts.astype(jnp.int32))
    shared = jax.random.fold_in(floor_value, 7)
    row_keys = jax.vmap(lambda index: jax.random.fold_in(shared, index))(jnp.arange(N_DOC))
    return jax.vmap(one_row)(row_keys, jnp.arange(N_DOC, dtype=jnp.int32))


def draw_block_owner(key, part):
    return block_lists(key)[0]


def draw_block_start(key, part):
    return block_lists(key)[1]


def draw_log_decay(key, part):
    complete_probe_vectors = jax.random.split(key, 5)
    floor_value = jnp.exp(jax.random.uniform(complete_probe_vectors[0], (1, ALL_WIDTH_SUM), minval=math.log(0.003), maxval=math.log(0.08)))
    devices = SEQUENCE_LENGTH // TOK_DEV
    multiplier_coefficient = jnp.exp(jax.random.uniform(complete_probe_vectors[1], (devices, 1, 1), minval=math.log(0.6), maxval=math.log(1.6)))
    multiplier_coefficient = jnp.broadcast_to(multiplier_coefficient, (devices, TOK_DEV, 1)).reshape(SEQUENCE_LENGTH, 1)
    noise_perturbation = jnp.exp(jax.random.uniform(complete_probe_vectors[2], (SEQUENCE_LENGTH, ALL_WIDTH_SUM), minval=-0.5, maxval=0.5))
    spike_occurrence = jax.random.uniform(complete_probe_vectors[3], (SEQUENCE_LENGTH, OWNED_PARTITION, 1)) < 0.006
    dispersion_width = jax.random.uniform(complete_probe_vectors[4], (SEQUENCE_LENGTH, OWNED_PARTITION, 1), minval=math.log(0.5), maxval=math.log(0.8))
    spike_occurrences = jnp.broadcast_to(jnp.where(spike_occurrence, dispersion_width, 0.0), (SEQUENCE_LENGTH, OWNED_PARTITION, PER_QUERY_WIDTH)).reshape(SEQUENCE_LENGTH, ALL_WIDTH_SUM)
    return (spike_occurrences - floor_value * multiplier_coefficient * noise_perturbation).astype(jnp.float32).astype(jnp.bfloat16)


def level_of(stream_key, shape, pieces, smallest, high):
    def one(dim, shards_of):
        draws = jax.random.uniform(jax.random.fold_in(jax.random.fold_in(stream_key, 6), dim), (shards_of,), jnp.float32, smallest / len(pieces), high / len(pieces))
        return jnp.repeat(jnp.exp(draws), shape[dim] // shards_of).reshape((-1,) + (1,) * (len(shape) - dim - 1))

    level = one(*pieces[0])
    for cut in pieces[1:]:
        level = level * one(*cut)
    return level


def gaussian(stream_key, dims, scale, most, cuts=(), kind=jnp.bfloat16):
    values = scale * jax.random.normal(stream_key, dims, jnp.float32)
    if cuts:
        values = values * level_of(stream_key, dims, cuts, -0.22, 0.18)
    return jnp.clip(values, -most, most).astype(kind)


def setup_inputs(seed: int = 0) -> dict:
    streams_of = jax.random.split(jax.random.key(seed), 9)
    queries = gaussian(streams_of[0], (SEQUENCE_LENGTH, ALL_WIDTH_SUM), 1.0, 6.0, ((0, 32),))
    keys = gaussian(streams_of[1], (SEQUENCE_LENGTH, ALL_WIDTH_SUM), 1.0, 6.0, ((0, 32),))
    values = gaussian(streams_of[2], (SEQUENCE_LENGTH, ALL_WIDTH_SUM), 1.0, 6.0, ((0, 32),))
    log_decay = draw_log_decay(jax.random.fold_in(streams_of[8], 71), 0)
    beta_logit = gaussian(streams_of[4], (SEQUENCE_LENGTH, OWNED_PARTITION), 1.5, 6.0, ((0, 32),))
    block_owner = draw_block_owner(jax.random.fold_in(streams_of[8], 71), 0)
    block_start = draw_block_start(jax.random.fold_in(streams_of[8], 71), 0)
    gain = jnp.clip(1.0 + 0.15 * jax.random.normal(streams_of[7], (ALL_WIDTH_SUM,), jnp.float32), 0.25, 1.75)
    return {"queries": queries, "keys": keys, "values": values, "log_decay": log_decay, "beta_logit": beta_logit, "block_owner": block_owner, "block_start": block_start, "gain": gain}


HIGH = lax.Precision.HIGHEST

def unit_lower_inverse(amat):
    tile = amat.shape[-1]
    negated = -amat
    inverse = jnp.eye(tile, dtype=jnp.float32)[None] + negated
    power = negated
    for level in range(tile.bit_length() - 2):
        power = jnp.einsum('nts,nsr->ntr', power, power, precision=HIGH)
        inverse = inverse + jnp.einsum('nts,nsr->ntr', inverse, power, precision=HIGH)
    return inverse

def recurrence(query, key_in, value, decay, beta_raw, start):
    length, width = query.shape
    count = length // TILE
    query_f = query.astype(jnp.float32)
    keys_f = key_in.astype(jnp.float32)
    query_f = query_f * lax.rsqrt(lax.optimization_barrier(jnp.sum(query_f * query_f, axis=-1, keepdims=True)) + 1e-06) * width ** (-0.5)
    keys_f = keys_f * lax.rsqrt(lax.optimization_barrier(jnp.sum(keys_f * keys_f, axis=-1, keepdims=True)) + 1e-06)
    query_f = query_f.reshape(count, TILE, width)
    keys_f = keys_f.reshape(count, TILE, width)
    values_f = value.astype(jnp.float32).reshape(count, TILE, width)
    beta = jax.nn.sigmoid(beta_raw.astype(jnp.float32)).reshape(count, TILE, 1)
    decay_f = decay.astype(jnp.float32).reshape(count, TILE, width)
    row_idx = lax.broadcasted_iota(jnp.int32, (TILE, TILE), 0)
    col_idx = lax.broadcasted_iota(jnp.int32, (TILE, TILE), 1)
    lower_incl = row_idx >= col_idx
    lower_strict = row_idx > col_idx
    cumul = jnp.einsum('ts,nsd->ntd', lower_incl.astype(jnp.float32), decay_f, precision=HIGH)
    segment = jnp.cumsum(start.reshape(count, TILE).astype(jnp.int32), axis=1)
    first = (segment == 0).astype(jnp.float32)[:, :, None]
    last_seg = (segment == segment[:, -1:]).astype(jnp.float32)[:, :, None]
    same = segment[:, :, None] == segment[:, None, :]
    growth = jnp.exp(cumul)
    query_g = query_f * growth
    keys_g = keys_f * growth
    keys_inv = keys_f * jnp.exp(-cumul)
    inner = jnp.einsum('ntd,nsd->nts', keys_g, keys_inv, precision=HIGH)
    amat = jnp.where(same & lower_strict, inner, 0.0) * beta
    scores = jnp.where(same & lower_incl, jnp.einsum('ntd,nsd->nts', query_g, keys_inv, precision=HIGH), 0.0)
    right = jnp.concatenate([beta * values_f, beta * first * keys_g], axis=-1)
    solved = jnp.einsum('nts,nse->nte', unit_lower_inverse(amat), right, precision=HIGH)
    update_free = solved[:, :, :width]
    update_state = solved[:, :, width:]
    keys_end = keys_f * jnp.exp(cumul[:, -1:, :] - cumul) * last_seg
    carry_scale = first[:, -1, :] * growth[:, -1, :]
    transfer = jnp.eye(width, dtype=jnp.float32)[None] * carry_scale[:, :, None] - jnp.einsum('nsd,nse->nde', keys_end, update_state, precision=HIGH)
    offset = jnp.einsum('nsd,nse->nde', keys_end, update_free, precision=HIGH)

    def advance(state, pair):
        return (jnp.dot(pair[0], state, precision=HIGH) + pair[1], state)
    unused, states = lax.scan(advance, jnp.zeros((width, width), jnp.float32), (transfer, offset))
    readout = first * query_g - jnp.einsum('nts,nsd->ntd', scores, update_state, precision=HIGH)
    result = jnp.einsum('ntd,nde->nte', readout, states, precision=HIGH) + jnp.einsum('nts,nse->nte', scores, update_free, precision=HIGH)
    return result.reshape(length, width)

def normalize(result, gain):
    heads_here = result.shape[1]
    scale = lax.rsqrt(lax.optimization_barrier(jnp.mean(result * result, axis=-1, keepdims=True)) + 1e-05)
    normed = result * scale * gain.reshape(1, heads_here, PER_QUERY_WIDTH)
    return normed.reshape(result.shape[0], heads_here * PER_QUERY_WIDTH).astype(jnp.bfloat16)

def reference(queries, keys, values, log_decay, beta_logit, block_owner, block_start, gain):
    first_tok = (jnp.arange(BLOCK) == 0).astype(jnp.int32)
    token_start = (block_start[:, :, None] * first_tok[None, None, :]).reshape(N_DOC, ROWTOK)
    run_heads = jax.vmap(recurrence, in_axes=(1, 1, 1, 1, 1, None), out_axes=1)

    def row_out(items):
        query_row, key_row, value_row, decay_row, beta_row, start_row = items
        shaped = [item.reshape(ROWTOK, OWNED_PARTITION, PER_QUERY_WIDTH) for item in (query_row, key_row, value_row, decay_row)]
        result = run_heads(shaped[0], shaped[1], shaped[2], shaped[3], beta_row, start_row)
        return normalize(result, gain)
    rows_out = lax.map(row_out, (queries.reshape(N_DOC, ROWTOK, ALL_WIDTH_SUM), keys.reshape(N_DOC, ROWTOK, ALL_WIDTH_SUM), values.reshape(N_DOC, ROWTOK, ALL_WIDTH_SUM), log_decay.reshape(N_DOC, ROWTOK, ALL_WIDTH_SUM), beta_logit.reshape(N_DOC, ROWTOK, OWNED_PARTITION), token_start))
    earlier = (jnp.arange(RB)[None, :] < jnp.arange(RB)[:, None]).astype(jnp.int32)
    matches = (block_owner[:, :, None] == block_owner[:, None, :]).astype(jnp.int32)
    ranks = lax.optimization_barrier(jnp.sum(matches * earlier[None], axis=2)).astype(jnp.int32)
    rows_index = jnp.arange(N_DOC, dtype=jnp.int32)[:, None]
    offsets = jnp.mod(block_owner - rows_index + N_DOC, N_DOC).astype(jnp.int32)
    target = (block_owner * (RUNS * CAP) + offsets * CAP + ranks).astype(jnp.int32)
    placed = jnp.zeros((N_DOC * RUNS * CAP, BLOCK, ALL_WIDTH_SUM), jnp.bfloat16)
    placed = placed.at[target.reshape(-1)].set(rows_out.reshape(N_DOC * RB, BLOCK, ALL_WIDTH_SUM))
    return placed.reshape(N_DOC * OS, ALL_WIDTH_SUM)
```

```python
import functools

import jax
import jax.numpy as jnp
from jax import lax
from jax.experimental import pallas as pl
from jax.experimental.pallas import tpu as pltpu
from jax.sharding import PartitionSpec as P

WIDTH = 128
BLOCK = 16
TILE = 128
RUNS = 4
BASE = 16

MESH = pl.DeviceIdType.MESH
F32 = jnp.float32
BF16 = jnp.bfloat16
NN = (((1,), (0,)), ((), ()))
NT = (((1,), (1,)), ((), ()))
TN = (((0,), (0,)), ((), ()))


def split(x):
    high = x.astype(BF16)
    return high, (x - high.astype(F32)).astype(BF16)


def bdot(a, b, dims=NN):
    return lax.dot_general(a, b, dims, preferred_element_type=F32)


def dot3(a, b, dims=NN):
    a_high, a_low = split(a) if not isinstance(a, tuple) else a
    b_high, b_low = split(b) if not isinstance(b, tuple) else b
    ca, cb = dims[0][0][0], dims[0][1][0]
    left = jnp.concatenate([a_high, a_low], axis=ca)
    free = 1 - cb
    top = jnp.concatenate([b_high, b_low], axis=free)
    bottom = jnp.concatenate([b_high, jnp.zeros_like(b_low)], axis=free)
    both = bdot(left, jnp.concatenate([top, bottom], axis=cb), dims)
    width = both.shape[1] // 2
    return both[:, :width] + both[:, width:]


def lane_iota(shape):
    return lax.broadcasted_iota(jnp.int32, shape, 1)


def row_iota(shape):
    return lax.broadcasted_iota(jnp.int32, shape, 0)


def neumann(neg, order, eye):
    power = [dot3(n, n) for n in neg]
    total = [eye + n for n in neg]
    size = 2
    while size < order:
        if size * 2 >= order:
            total = [x + dot3(x, p) for x, p in zip(total, power)]
        else:
            both = [dot3(jnp.concatenate([x, p], axis=0), p) for x, p in zip(total, power)]
            total = [x + b[:TILE] for x, b in zip(total, both)]
            power = [b[TILE:] for b in both]
        size *= 2
    return total


def inverses(mats):
    shape = (TILE, TILE)
    row, col = row_iota(shape), lane_iota(shape)
    eye = (row == col).astype(F32)
    diag = row // BASE == col // BASE
    inner = neumann([jnp.where(diag, -a, 0.0) for a in mats], BASE, eye)
    parts = [split(x) for x in inner]
    outer = [-dot3(p, jnp.where(diag, 0.0, a)) for p, a in zip(parts, mats)]
    return [dot3(y, p) for y, p in zip(neumann(outer, TILE // BASE, eye), parts)]


def rows_of(steps, body):
    if steps <= 4:
        for step in range(steps):
            body(step)
    else:
        lax.fori_loop(0, steps, lambda step, carry: (body(step), carry)[1], 0)


def kernel(
    nz, nd, parcels, q_ref, k_ref, v_ref, g_ref, b_ref, owner_in, start_in, gain_in, out_ref,
    buf, held, bbuf, owner_ref, start_ref, gain_ref, betas, brows, place, stage, segcol, masks,
    growth, keyinv, keystate, halves, weights, ends, carries, mats, placed,
    local_sem, send_sem, recv_sem, bsend_sem, brecv_sem, osend_sem, orecv_sem,
):
    me = lax.axis_index("head")
    doc = lax.axis_index("doc")
    _, rowtok, columns = buf.shape
    heads = columns // WIDTH
    tok = q_ref.shape[0]
    nblk = rowtok // BLOCK
    cap = 2 * nblk // RUNS
    capt = cap * BLOCK
    tiles = rowtok // TILE
    slots = RUNS * capt
    shape = (TILE, TILE)
    refs = (k_ref, g_ref, q_ref, v_ref)

    barrier = pltpu.get_barrier_semaphore()
    count = 0
    for step in range(1, nz):
        pl.semaphore_signal(
            barrier, inc=1, device_id={"head": lax.rem(me + step, nz)}, device_id_type=MESH
        )
        count += 1
    peers = sorted({s % nd for s in range(1, RUNS)} | {(-s) % nd for s in range(1, RUNS)})
    for step in peers:
        pl.semaphore_signal(
            barrier, inc=1, device_id={"doc": lax.rem(doc + step, nd)}, device_id_type=MESH
        )
        count += 1

    mine = pl.ds(pl.multiple_of(me * tok, tok), tok)
    own = pl.ds(pl.multiple_of(me * columns, columns), columns)
    fetch = [pltpu.make_async_copy(refs[w], held.at[w], local_sem.at[w]) for w in range(4)]
    small = [
        pltpu.make_async_copy(source, target, local_sem.at[4 + index])
        for index, (source, target) in enumerate(
            [(owner_in, owner_ref), (start_in, start_ref), (gain_in, gain_ref), (b_ref, bbuf.at[me])]
        )
    ]
    keep = [
        pltpu.make_async_copy(refs[w].at[:, own], buf.at[w, mine, :], local_sem.at[8 + w])
        for w in range(4)
    ]
    for copy in fetch + small + keep:
        copy.start()
    for copy in fetch:
        copy.wait()
    pl.semaphore_wait(barrier, count)

    def incoming(step, parcel):
        (first, last), (low, high) = parcels[parcel]
        partner = lax.rem(me + step, nz)
        begin = pl.multiple_of(partner * columns + low * WIDTH, WIDTH)
        return pltpu.make_async_remote_copy(
            src_ref=held.at[first:last, :, pl.ds(begin, (high - low) * WIDTH)],
            dst_ref=buf.at[first:last, mine, low * WIDTH : high * WIDTH],
            send_sem=send_sem.at[step, parcel],
            recv_sem=recv_sem.at[step, parcel],
            device_id={"head": partner},
            device_id_type=MESH,
        )

    def incoming_beta(step):
        return pltpu.make_async_remote_copy(
            src_ref=b_ref,
            dst_ref=bbuf.at[me],
            send_sem=bsend_sem.at[step],
            recv_sem=brecv_sem.at[step],
            device_id={"head": lax.rem(me + step, nz)},
            device_id_type=MESH,
        )

    def outgoing(run, head):
        rows = pl.ds(run * capt, capt)
        return pltpu.make_async_remote_copy(
            src_ref=stage.at[head, rows, :],
            dst_ref=out_ref.at[rows, pl.ds(pl.multiple_of(head * WIDTH, WIDTH), WIDTH)],
            send_sem=osend_sem.at[run, head],
            recv_sem=orecv_sem.at[run, head],
            device_id={"doc": lax.rem(doc + run, nd)},
            device_id_type=MESH,
        )

    steps = sorted(range(1, nz), key=lambda s: (-min(s, nz - s), s))
    for step in steps:
        incoming_beta(step).start()
    for parcel in range(len(parcels)):
        for step in steps:
            incoming(step, parcel).start()

    for copy in small:
        copy.wait()
    here = row_iota((nd, nblk)) == doc
    owner = jnp.sum(jnp.where(here, owner_ref[...], 0), axis=0, keepdims=True)
    start = jnp.sum(jnp.where(here, start_ref[...], 0), axis=0, keepdims=True)
    eye_b = row_iota((nblk, nblk)) == lane_iota((nblk, nblk))
    owner_col = jnp.sum(jnp.where(eye_b, owner, 0), axis=1, keepdims=True)
    earlier = row_iota((nblk, nblk)) < lane_iota((nblk, nblk))
    rank = jnp.sum(jnp.where(earlier & (owner_col == owner), 1, 0), axis=0, keepdims=True)
    ahead = owner - doc
    ahead = jnp.where(ahead < 0, ahead + nd, ahead)
    slot = (ahead * cap + rank).astype(F32).astype(BF16)
    token_block = lane_iota((nblk, rowtok)) // BLOCK
    expand = (row_iota((nblk, rowtok)) == token_block).astype(F32).astype(BF16)
    slot_tok = bdot(slot, expand).astype(jnp.int32) * BLOCK + lane_iota((1, rowtok)) % BLOCK
    place[...] = (row_iota((slots, rowtok)) == slot_tok).astype(F32).astype(BF16)
    upto = (row_iota((nblk, rowtok)) <= token_block).astype(F32).astype(BF16)
    seg_row = bdot(start.astype(F32).astype(BF16), upto)
    seg_col = jnp.sum(
        jnp.where(
            lane_iota((rowtok, nblk)) <= row_iota((rowtok, nblk)) // BLOCK, start.astype(F32), 0.0
        ),
        axis=1,
        keepdims=True,
    )
    segcol[...] = jnp.broadcast_to(seg_col, (rowtok, WIDTH))
    for tile in range(tiles):
        lo = tile * TILE
        same = seg_col[lo : lo + TILE] == seg_row[:, lo : lo + TILE]
        masks[tile, 0] = (same & (row_iota(shape) > lane_iota(shape))).astype(F32)
        masks[tile, 1] = (same & (row_iota(shape) >= lane_iota(shape))).astype(F32)
    for tile in range(tiles - 1):
        lo = tile * TILE
        for half in range(2):
            wide = pl.ds(half * rowtok + lo + TILE, rowtok - lo - TILE)
            mats[:, lo : lo + TILE, wide] = jnp.zeros(
                (mats.shape[0], TILE, rowtok - lo - TILE), BF16
            )

    for step in range(1, nz):
        incoming_beta(step).wait_recv()

    eye_tok = (row_iota((tok, tok)) == lane_iota((tok, tok))).astype(F32).astype(BF16)
    flat = jnp.zeros((bbuf.shape[1], rowtok), F32)
    for step in range(nz):
        turned = bdot(eye_tok, bbuf[step], NT)
        betas[step * tok : (step + 1) * tok, :] = jax.nn.sigmoid(turned)
        shift = row_iota((tok, rowtok)) + step * tok == lane_iota((tok, rowtok))
        flat = flat + bdot(bbuf[step], shift.astype(F32).astype(BF16))
    brows[...] = jax.nn.sigmoid(flat)

    for copy in keep:
        copy.wait()

    def arrive(parcel):
        for step in range(1, nz):
            incoming(step, parcel).wait_recv()

    def beta_of(head):
        values = betas[...]
        mine_here = lane_iota(values.shape) == me * heads + head
        return jnp.sum(jnp.where(mine_here, values, 0.0), axis=1, keepdims=True)

    def before(tile):
        return segcol[tile * TILE - 1 : tile * TILE, :]

    def final(tile):
        return segcol[(tile + 1) * TILE - 1 : (tile + 1) * TILE, :]

    def lanes(head):
        return pl.ds(head * WIDTH, WIDTH)

    def keys_part(members):
        lower = (row_iota(shape) >= lane_iota(shape)).astype(F32).astype(BF16)
        where, amats, tails = [], [], []
        for head in members:
            beta = beta_of(head)
            for tile in range(tiles):
                rows = pl.ds(tile * TILE, TILE)
                seg = segcol[rows, :]
                key = buf[0, rows, lanes(head)].astype(F32)
                key = key * lax.rsqrt(jnp.sum(key * key, axis=-1, keepdims=True) + 1e-06)
                cumul = bdot(lower, buf[1, rows, lanes(head)])
                half = 0.5 * cumul[TILE - 1 :, :]
                grow = jnp.exp(cumul - half)
                middle = jnp.exp(half)
                kg, ki = key * grow, key * jnp.exp(half - cumul)
                amat = dot3(kg, ki, NT)
                amat = jnp.where(masks[tile, 0] > 0.0, amat, 0.0)
                amats.append(amat * beta[tile * TILE : (tile + 1) * TILE])
                where.append((head, tile, rows))
                growth[head, rows, :] = grow
                keyinv[head, rows, :] = ki
                halves[head, tile] = jnp.broadcast_to(middle, (8, WIDTH))
                if tile > 0:
                    keystate[head, rows, :] = kg * ((seg == before(tile)).astype(F32) * middle)
                tails.append(ki * ((seg == final(tile)).astype(F32) * middle))
        solved = []
        for (head, tile, rows), inv in zip(where, inverses(amats)):
            row = brows[pl.ds(me * heads + head, 1), :]
            scaled = inv * row[:, tile * TILE : (tile + 1) * TILE]
            weights[head, rows, :] = scaled
            solved.append(scaled)
        made = [
            dot3(t, w, TN) if tile < tiles - 1 else None
            for (head, tile, rows), t, w in zip(where, tails, solved)
        ]
        for (head, tile, rows), end in zip(where, made):
            if tile < tiles - 1:
                ends[head, tile] = end
                if tile > 0:
                    middle = halves[head, tile, 0:1, :]
                    scale = middle * middle * (final(tile) == before(tile)).astype(F32)
                    eye = row_iota(shape) == lane_iota(shape)
                    carries[head, tile] = jnp.where(eye, scale, 0.0) - dot3(
                        end, keystate[head, rows, :]
                    )

    def store(index, tile, source, block):
        high, low = split(block)
        rows = pl.ds(tile * TILE, TILE)
        mats[index, rows, pl.ds(source * TILE, TILE)] = high
        mats[index, rows, pl.ds(rowtok + source * TILE, TILE)] = low

    def queries_part(members):
        where, grown, scores = [], [], []
        for index, head in enumerate(members):
            for tile in range(tiles):
                rows = pl.ds(tile * TILE, TILE)
                query = buf[2, rows, lanes(head)].astype(F32)
                query = (
                    query
                    * lax.rsqrt(jnp.sum(query * query, axis=-1, keepdims=True) + 1e-06)
                    * WIDTH ** (-0.5)
                )
                qg = query * growth[head, rows, :]
                score = dot3(qg, keyinv[head, rows, :], NT)
                scores.append(jnp.where(masks[tile, 1] > 0.0, score, 0.0))
                grown.append(qg)
                where.append((index, head, tile, rows))
        inner = [
            dot3(score, weights[head, rows, :])
            for (index, head, tile, rows), score in zip(where, scores)
        ]
        reads = []
        for (index, head, tile, rows), block, qg in zip(where, inner, grown):
            store(index, tile, tile, block)
            if tile > 0:
                first = (segcol[rows, :] == before(tile)).astype(F32) * halves[head, tile, 0:1, :]
                reads.append(qg * first - dot3(block, keystate[head, rows, :]))
            else:
                reads.append(None)
        for index, head in enumerate(members):
            for source in range(tiles - 1):
                state = ends[head, source]
                for tile in range(source + 1, tiles):
                    parts = split(state)
                    store(index, tile, source, dot3(reads[index * tiles + tile], parts))
                    if tile < tiles - 1:
                        state = dot3(carries[head, tile], parts)
        for index, head in enumerate(members):

            def move(step):
                rows = pl.ds(pl.multiple_of(step * TILE, TILE), TILE)
                placed[head, rows, :] = bdot(place[rows, :], mats[index]).astype(BF16)

            rows_of(slots // TILE, move)

    def values_part(head):
        value = buf[3, :, lanes(head)]
        value = jnp.concatenate([value, value], axis=0)
        gain = gain_ref[:, lanes(head)]
        for run in list(range(1, RUNS)) + [0]:
            rows = pl.ds(run * capt, capt)
            result = bdot(placed[head, rows, :], value)
            norm = lax.rsqrt(jnp.mean(result * result, axis=-1, keepdims=True) + 1e-05)
            result = (result * norm * gain).astype(BF16)
            if run == 0:
                out_ref[rows, lanes(head)] = result
            else:
                stage[head, rows, :] = result
                outgoing(run, head).start()

    group = mats.shape[0]
    for parcel, ((first, last), (low, high)) in enumerate(parcels):
        arrive(parcel)
        for begin in range(low, high, group):
            members = list(range(begin, min(begin + group, high)))
            if first == 0:
                keys_part(members)
            if first <= 2 < last:
                queries_part(members)
        if last == 4:
            for head in range(low, high):
                values_part(head)

    for step in range(1, nz):
        incoming_beta(step).wait_send()
        for parcel in range(len(parcels)):
            incoming(step, parcel).wait_send()
    for head in range(heads):
        for run in range(1, RUNS):
            outgoing(run, head).wait()


def parcels_of(heads):
    group = 2 if heads % 2 == 0 else 1
    pairs = [(low, low + group) for low in range(0, heads, group)]
    return (
        [((0, 2), pair) for pair in pairs]
        + [((2, 3), pair) for pair in pairs]
        + [((3, 4), (head, head + 1)) for head in range(heads)]
    )


def solution(mesh):
    nz, nd = mesh.shape["head"], mesh.shape["doc"]

    def local(queries, keys, values, log_decay, beta_logit, block_owner, block_start, gain):
        tok, channels = queries.shape
        heads = channels // WIDTH // nz
        rowtok = tok * nz
        slots = 2 * rowtok
        tiles = rowtok // TILE
        group = 2 if heads % 2 == 0 else 1
        parcels = parcels_of(heads)
        anywhere = pl.BlockSpec(memory_space=pl.ANY)
        dma = pltpu.SemaphoreType.DMA
        return pl.pallas_call(
            functools.partial(kernel, nz, nd, parcels),
            out_shape=pltpu.VMEM((slots, heads * WIDTH), BF16),
            in_specs=[anywhere] * 8,
            out_specs=pl.BlockSpec(memory_space=pltpu.VMEM),
            scratch_shapes=[
                pltpu.VMEM((4, rowtok, heads * WIDTH), BF16),
                pltpu.VMEM((4, tok, channels), BF16),
                pltpu.VMEM((nz, beta_logit.shape[1], tok), BF16),
                pltpu.VMEM(block_owner.shape, jnp.int32),
                pltpu.VMEM(block_start.shape, jnp.int32),
                pltpu.VMEM((1, heads * WIDTH), F32),
                pltpu.VMEM((rowtok, beta_logit.shape[1]), F32),
                pltpu.VMEM((beta_logit.shape[1], rowtok), F32),
                pltpu.VMEM((slots, rowtok), BF16),
                pltpu.VMEM((heads, slots, WIDTH), BF16),
                pltpu.VMEM((rowtok, WIDTH), F32),
                pltpu.VMEM((tiles, 2, TILE, TILE), F32),
                pltpu.VMEM((heads, rowtok, WIDTH), F32),
                pltpu.VMEM((heads, rowtok, WIDTH), F32),
                pltpu.VMEM((heads, rowtok, WIDTH), F32),
                pltpu.VMEM((heads, tiles, 8, WIDTH), F32),
                pltpu.VMEM((heads, rowtok, WIDTH), F32),
                pltpu.VMEM((heads, tiles, WIDTH, WIDTH), F32),
                pltpu.VMEM((heads, tiles, WIDTH, WIDTH), F32),
                pltpu.VMEM((group, rowtok, 2 * rowtok), BF16),
                pltpu.VMEM((heads, slots, 2 * rowtok), BF16),
                dma((12,)),
                dma((nz, len(parcels))),
                dma((nz, len(parcels))),
                dma((nz,)),
                dma((nz,)),
                dma((RUNS, heads)),
                dma((RUNS, heads)),
            ],
            compiler_params=pltpu.CompilerParams(
                collective_id=0, has_side_effects=True, vmem_limit_bytes=60 * 1024 * 1024
            ),
            name="delta",
        )(
            queries, keys, values, log_decay, beta_logit.T, block_owner, block_start,
            gain.reshape(1, -1),
        )

    return jax.shard_map(
        local,
        mesh=mesh,
        in_specs=(P(("doc", "head"), None),) * 5 + (P(), P(), P("head")),
        out_specs=P("doc", "head"),
        check_vma=False,
    )
```

```python
import functools

import jax
import jax.numpy as jnp
from jax import lax
from jax.experimental import pallas as pl
from jax.experimental.pallas import tpu as pltpu
from jax.sharding import PartitionSpec as P

WIDTH = 128
BLOCK = 16
TILE = 128
RUNS = 4
BASE = 16
AHEAD = 3

MESH = pl.DeviceIdType.MESH
F32 = jnp.float32
BF16 = jnp.bfloat16
NN = (((1,), (0,)), ((), ()))
NT = (((1,), (1,)), ((), ()))
TN = (((0,), (0,)), ((), ()))


def split(x):
    high = x.astype(BF16)
    return high, (x - high.astype(F32)).astype(BF16)


def bdot(a, b, dims=NN):
    return lax.dot_general(a, b, dims, preferred_element_type=F32)


def dot3(a, b, dims=NN):
    a_high, a_low = split(a) if not isinstance(a, tuple) else a
    b_high, b_low = split(b) if not isinstance(b, tuple) else b
    ca, cb = dims[0][0][0], dims[0][1][0]
    left = jnp.concatenate([a_high, a_low], axis=ca)
    free = 1 - cb
    top = jnp.concatenate([b_high, b_low], axis=free)
    bottom = jnp.concatenate([b_high, jnp.zeros_like(b_low)], axis=free)
    both = bdot(left, jnp.concatenate([top, bottom], axis=cb), dims)
    width = both.shape[1] // 2
    return both[:, :width] + both[:, width:]


def lane_iota(shape):
    return lax.broadcasted_iota(jnp.int32, shape, 1)


def row_iota(shape):
    return lax.broadcasted_iota(jnp.int32, shape, 0)


def neumann(neg, order, eye):
    power = [dot3(n, n) for n in neg]
    total = [eye + n for n in neg]
    size = 2
    while size < order:
        if size * 2 >= order:
            total = [x + dot3(x, p) for x, p in zip(total, power)]
        else:
            both = [dot3(jnp.concatenate([x, p], axis=0), p) for x, p in zip(total, power)]
            total = [x + b[:TILE] for x, b in zip(total, both)]
            power = [b[TILE:] for b in both]
        size *= 2
    return total


def inverses(mats):
    shape = (TILE, TILE)
    row, col = row_iota(shape), lane_iota(shape)
    eye = (row == col).astype(F32)
    diag = row // BASE == col // BASE
    inner = neumann([jnp.where(diag, -a, 0.0) for a in mats], BASE, eye)
    parts = [split(x) for x in inner]
    outer = [-dot3(p, jnp.where(diag, 0.0, a)) for p, a in zip(parts, mats)]
    return [dot3(y, p) for y, p in zip(neumann(outer, TILE // BASE, eye), parts)]


def rows_of(steps, body):
    if steps <= 4:
        for step in range(steps):
            body(step)
    else:
        lax.fori_loop(0, steps, lambda step, carry: (body(step), carry)[1], 0)


def kernel(
    nz, nd, parcels, q_ref, k_ref, v_ref, g_ref, b_ref, owner_in, start_in, gain_in, out_ref,
    buf, held, bbuf, owner_ref, start_ref, gain_ref, betas, brows, place, stage, segcol, masks,
    growth, keyinv, keystate, halves, weights, ends, carries, mats, placed,
    local_sem, send_sem, recv_sem, bsend_sem, brecv_sem, osend_sem, orecv_sem,
    row_sem, all_sem,
):
    me = lax.axis_index("head")
    doc = lax.axis_index("doc")
    _, rowtok, columns = buf.shape
    heads = columns // WIDTH
    tok = q_ref.shape[0]
    nblk = rowtok // BLOCK
    cap = 2 * nblk // RUNS
    capt = cap * BLOCK
    tiles = rowtok // TILE
    slots = RUNS * capt
    shape = (TILE, TILE)
    refs = (k_ref, g_ref, q_ref, v_ref)

    def greet(semaphore):
        for step in peers:
            pl.semaphore_signal(
                semaphore, inc=1, device_id={"doc": lax.rem(doc + step, nd)}, device_id_type=MESH
            )

    barrier = pltpu.get_barrier_semaphore()
    count = 0
    for step in range(1, nz):
        pl.semaphore_signal(
            barrier, inc=1, device_id={"head": lax.rem(me + step, nz)}, device_id_type=MESH
        )
        count += 1
    peers = sorted({s % nd for s in range(1, RUNS)} | {(-s) % nd for s in range(1, RUNS)})
    leader = me == 0

    @pl.when(leader)
    def _():
        greet(barrier)


    mine = pl.ds(pl.multiple_of(me * tok, tok), tok)
    own = pl.ds(pl.multiple_of(me * columns, columns), columns)
    fetch = [pltpu.make_async_copy(refs[w], held.at[w], local_sem.at[w]) for w in range(4)]
    small = [
        pltpu.make_async_copy(source, target, local_sem.at[4 + index])
        for index, (source, target) in enumerate(
            [(owner_in, owner_ref), (start_in, start_ref), (gain_in, gain_ref), (b_ref, bbuf.at[me])]
        )
    ]
    keep = [
        pltpu.make_async_copy(refs[w].at[:, own], buf.at[w, mine, :], local_sem.at[8 + w])
        for w in range(4)
    ]
    for copy in fetch + small + keep:
        copy.start()
    for copy in fetch:
        copy.wait()

    @pl.when(leader)
    def _():
        pl.semaphore_wait(barrier, count + len(peers))
        greet(row_sem)

    @pl.when(me != 0)
    def _():
        pl.semaphore_wait(barrier, count)

    def incoming(step, parcel):
        (first, last), (low, high) = parcels[parcel]
        partner = lax.rem(me + step, nz)
        begin = pl.multiple_of(partner * columns + low * WIDTH, WIDTH)
        return pltpu.make_async_remote_copy(
            src_ref=held.at[first:last, :, pl.ds(begin, (high - low) * WIDTH)],
            dst_ref=buf.at[first:last, mine, low * WIDTH : high * WIDTH],
            send_sem=send_sem.at[step, parcel],
            recv_sem=recv_sem.at[step, parcel],
            device_id={"head": partner},
            device_id_type=MESH,
        )

    def incoming_beta(step):
        return pltpu.make_async_remote_copy(
            src_ref=b_ref,
            dst_ref=bbuf.at[me],
            send_sem=bsend_sem.at[step],
            recv_sem=brecv_sem.at[step],
            device_id={"head": lax.rem(me + step, nz)},
            device_id_type=MESH,
        )

    def outgoing(run, head):
        rows = pl.ds(run * capt, capt)
        return pltpu.make_async_remote_copy(
            src_ref=stage.at[head, rows, :],
            dst_ref=out_ref.at[rows, pl.ds(pl.multiple_of(head * WIDTH, WIDTH), WIDTH)],
            send_sem=osend_sem.at[run, head],
            recv_sem=orecv_sem.at[run, head],
            device_id={"doc": lax.rem(doc + run, nd)},
            device_id_type=MESH,
        )

    steps = sorted(range(1, nz), key=lambda s: (-min(s, nz - s), s))
    for step in steps:
        incoming_beta(step).start()
    for parcel in range(min(AHEAD, len(parcels))):
        for step in steps:
            incoming(step, parcel).start()

    for copy in small:
        copy.wait()
    here = row_iota((nd, nblk)) == doc
    owner = jnp.sum(jnp.where(here, owner_ref[...], 0), axis=0, keepdims=True)
    start = jnp.sum(jnp.where(here, start_ref[...], 0), axis=0, keepdims=True)
    eye_b = row_iota((nblk, nblk)) == lane_iota((nblk, nblk))
    owner_col = jnp.sum(jnp.where(eye_b, owner, 0), axis=1, keepdims=True)
    earlier = row_iota((nblk, nblk)) < lane_iota((nblk, nblk))
    rank = jnp.sum(jnp.where(earlier & (owner_col == owner), 1, 0), axis=0, keepdims=True)
    ahead = owner - doc
    ahead = jnp.where(ahead < 0, ahead + nd, ahead)
    slot = (ahead * cap + rank).astype(F32).astype(BF16)
    token_block = lane_iota((nblk, rowtok)) // BLOCK
    expand = (row_iota((nblk, rowtok)) == token_block).astype(F32).astype(BF16)
    slot_tok = bdot(slot, expand).astype(jnp.int32) * BLOCK + lane_iota((1, rowtok)) % BLOCK
    place[...] = (row_iota((slots, rowtok)) == slot_tok).astype(F32).astype(BF16)
    upto = (row_iota((nblk, rowtok)) <= token_block).astype(F32).astype(BF16)
    seg_row = bdot(start.astype(F32).astype(BF16), upto)
    seg_col = jnp.sum(
        jnp.where(
            lane_iota((rowtok, nblk)) <= row_iota((rowtok, nblk)) // BLOCK, start.astype(F32), 0.0
        ),
        axis=1,
        keepdims=True,
    )
    segcol[...] = jnp.broadcast_to(seg_col, (rowtok, WIDTH))
    for tile in range(tiles):
        lo = tile * TILE
        same = seg_col[lo : lo + TILE] == seg_row[:, lo : lo + TILE]
        masks[tile, 0] = (same & (row_iota(shape) > lane_iota(shape))).astype(F32)
        masks[tile, 1] = (same & (row_iota(shape) >= lane_iota(shape))).astype(F32)
    for tile in range(tiles - 1):
        lo = tile * TILE
        for half in range(2):
            wide = pl.ds(half * rowtok + lo + TILE, rowtok - lo - TILE)
            mats[:, lo : lo + TILE, wide] = jnp.zeros(
                (mats.shape[0], TILE, rowtok - lo - TILE), BF16
            )

    for step in range(1, nz):
        incoming_beta(step).wait_recv()

    eye_tok = (row_iota((tok, tok)) == lane_iota((tok, tok))).astype(F32).astype(BF16)
    flat = jnp.zeros((bbuf.shape[1], rowtok), F32)
    for step in range(nz):
        turned = bdot(eye_tok, bbuf[step], NT)
        betas[step * tok : (step + 1) * tok, :] = jax.nn.sigmoid(turned)
        shift = row_iota((tok, rowtok)) + step * tok == lane_iota((tok, rowtok))
        flat = flat + bdot(bbuf[step], shift.astype(F32).astype(BF16))
    brows[...] = jax.nn.sigmoid(flat)

    for copy in keep:
        copy.wait()

    @pl.when(leader)
    def _():
        pl.semaphore_wait(row_sem, len(peers))
        for step in range(1, nz):
            pl.semaphore_signal(
                all_sem, inc=1, device_id={"head": lax.rem(me + step, nz)}, device_id_type=MESH
            )

    @pl.when(me != 0)
    def _():
        pl.semaphore_wait(all_sem, 1)

    def arrive(parcel):
        for step in range(1, nz):
            incoming(step, parcel).wait_recv()

    def beta_of(head):
        values = betas[...]
        mine_here = lane_iota(values.shape) == me * heads + head
        return jnp.sum(jnp.where(mine_here, values, 0.0), axis=1, keepdims=True)

    def before(tile):
        return segcol[tile * TILE - 1 : tile * TILE, :]

    def final(tile):
        return segcol[(tile + 1) * TILE - 1 : (tile + 1) * TILE, :]

    def lanes(head):
        return pl.ds(head * WIDTH, WIDTH)

    def keys_part(members):
        lower = (row_iota(shape) >= lane_iota(shape)).astype(F32).astype(BF16)
        where, amats, tails = [], [], []
        for head in members:
            beta = beta_of(head)
            for tile in range(tiles):
                rows = pl.ds(tile * TILE, TILE)
                seg = segcol[rows, :]
                key = buf[0, rows, lanes(head)].astype(F32)
                key = key * lax.rsqrt(jnp.sum(key * key, axis=-1, keepdims=True) + 1e-06)
                cumul = bdot(lower, buf[1, rows, lanes(head)])
                half = 0.5 * cumul[TILE - 1 :, :]
                grow = jnp.exp(cumul - half)
                middle = jnp.exp(half)
                kg, ki = key * grow, key * jnp.exp(half - cumul)
                amat = dot3(kg, ki, NT)
                amat = jnp.where(masks[tile, 0] > 0.0, amat, 0.0)
                amats.append(amat * beta[tile * TILE : (tile + 1) * TILE])
                where.append((head, tile, rows))
                growth[head, rows, :] = grow
                keyinv[head, rows, :] = ki
                halves[head, tile] = jnp.broadcast_to(middle, (8, WIDTH))
                if tile > 0:
                    keystate[head, rows, :] = kg * ((seg == before(tile)).astype(F32) * middle)
                tails.append(ki * ((seg == final(tile)).astype(F32) * middle))
        solved = []
        for (head, tile, rows), inv in zip(where, inverses(amats)):
            row = brows[pl.ds(me * heads + head, 1), :]
            scaled = inv * row[:, tile * TILE : (tile + 1) * TILE]
            weights[head, rows, :] = scaled
            solved.append(scaled)
        made = [
            dot3(t, w, TN) if tile < tiles - 1 else None
            for (head, tile, rows), t, w in zip(where, tails, solved)
        ]
        for (head, tile, rows), end in zip(where, made):
            if tile < tiles - 1:
                ends[head, tile] = end
                if tile > 0:
                    middle = halves[head, tile, 0:1, :]
                    scale = middle * middle * (final(tile) == before(tile)).astype(F32)
                    eye = row_iota(shape) == lane_iota(shape)
                    carries[head, tile] = jnp.where(eye, scale, 0.0) - dot3(
                        end, keystate[head, rows, :]
                    )

    def store(index, tile, source, block):
        high, low = split(block)
        rows = pl.ds(tile * TILE, TILE)
        mats[index, rows, pl.ds(source * TILE, TILE)] = high
        mats[index, rows, pl.ds(rowtok + source * TILE, TILE)] = low

    def queries_part(members):
        where, grown, scores = [], [], []
        for index, head in enumerate(members):
            for tile in range(tiles):
                rows = pl.ds(tile * TILE, TILE)
                query = buf[2, rows, lanes(head)].astype(F32)
                query = (
                    query
                    * lax.rsqrt(jnp.sum(query * query, axis=-1, keepdims=True) + 1e-06)
                    * WIDTH ** (-0.5)
                )
                qg = query * growth[head, rows, :]
                score = dot3(qg, keyinv[head, rows, :], NT)
                scores.append(jnp.where(masks[tile, 1] > 0.0, score, 0.0))
                grown.append(qg)
                where.append((index, head, tile, rows))
        inner = [
            dot3(score, weights[head, rows, :])
            for (index, head, tile, rows), score in zip(where, scores)
        ]
        reads = []
        for (index, head, tile, rows), block, qg in zip(where, inner, grown):
            store(index, tile, tile, block)
            if tile > 0:
                first = (segcol[rows, :] == before(tile)).astype(F32) * halves[head, tile, 0:1, :]
                reads.append(qg * first - dot3(block, keystate[head, rows, :]))
            else:
                reads.append(None)
        for index, head in enumerate(members):
            for source in range(tiles - 1):
                state = ends[head, source]
                for tile in range(source + 1, tiles):
                    parts = split(state)
                    store(index, tile, source, dot3(reads[index * tiles + tile], parts))
                    if tile < tiles - 1:
                        state = dot3(carries[head, tile], parts)
        for index, head in enumerate(members):

            def move(step):
                rows = pl.ds(pl.multiple_of(step * TILE, TILE), TILE)
                placed[head, rows, :] = bdot(place[rows, :], mats[index]).astype(BF16)

            rows_of(slots // TILE, move)

    def values_part(head):
        value = buf[3, :, lanes(head)]
        value = jnp.concatenate([value, value], axis=0)
        gain = gain_ref[:, lanes(head)]
        for run in list(range(2, RUNS)) + [1, 0]:
            rows = pl.ds(run * capt, capt)
            result = bdot(placed[head, rows, :], value)
            norm = lax.rsqrt(jnp.mean(result * result, axis=-1, keepdims=True) + 1e-05)
            result = (result * norm * gain).astype(BF16)
            if run == 0:
                out_ref[rows, lanes(head)] = result
            else:
                stage[head, rows, :] = result
                outgoing(run, head).start()

    group = mats.shape[0]
    for parcel, ((first, last), (low, high)) in enumerate(parcels):
        arrive(parcel)
        if parcel + AHEAD < len(parcels):
            for step in steps:
                incoming(step, parcel + AHEAD).start()
        for begin in range(low, high, group):
            members = list(range(begin, min(begin + group, high)))
            if first == 0:
                keys_part(members)
            if first <= 2 < last:
                queries_part(members)
        if last == 4:
            for head in range(low, high):
                values_part(head)

    for step in range(1, nz):
        incoming_beta(step).wait_send()
        for parcel in range(len(parcels)):
            incoming(step, parcel).wait_send()
    for head in range(heads):
        for run in range(1, RUNS):
            outgoing(run, head).wait()


def parcels_of(heads):
    group = 2 if heads % 2 == 0 else 1
    pairs = [(low, low + group) for low in range(0, heads, group)]
    return (
        [((0, 2), pair) for pair in pairs]
        + [part for pair in pairs[:-1] for part in (((2, 3), pair), ((3, 4), pair))]
        + [((2, 3), pairs[-1])]
        + [((3, 4), (head, head + 1)) for head in range(*pairs[-1])]
    )


def solution(mesh):
    nz, nd = mesh.shape["head"], mesh.shape["doc"]

    def local(queries, keys, values, log_decay, beta_logit, block_owner, block_start, gain):
        tok, channels = queries.shape
        heads = channels // WIDTH // nz
        rowtok = tok * nz
        slots = 2 * rowtok
        tiles = rowtok // TILE
        group = 2 if heads % 2 == 0 else 1
        parcels = parcels_of(heads)
        anywhere = pl.BlockSpec(memory_space=pl.ANY)
        dma = pltpu.SemaphoreType.DMA
        return pl.pallas_call(
            functools.partial(kernel, nz, nd, parcels),
            out_shape=pltpu.VMEM((slots, heads * WIDTH), BF16),
            in_specs=[anywhere] * 8,
            out_specs=pl.BlockSpec(memory_space=pltpu.VMEM),
            scratch_shapes=[
                pltpu.VMEM((4, rowtok, heads * WIDTH), BF16),
                pltpu.VMEM((4, tok, channels), BF16),
                pltpu.VMEM((nz, beta_logit.shape[1], tok), BF16),
                pltpu.VMEM(block_owner.shape, jnp.int32),
                pltpu.VMEM(block_start.shape, jnp.int32),
                pltpu.VMEM((1, heads * WIDTH), F32),
                pltpu.VMEM((rowtok, beta_logit.shape[1]), F32),
                pltpu.VMEM((beta_logit.shape[1], rowtok), F32),
                pltpu.VMEM((slots, rowtok), BF16),
                pltpu.VMEM((heads, slots, WIDTH), BF16),
                pltpu.VMEM((rowtok, WIDTH), F32),
                pltpu.VMEM((tiles, 2, TILE, TILE), F32),
                pltpu.VMEM((heads, rowtok, WIDTH), F32),
                pltpu.VMEM((heads, rowtok, WIDTH), F32),
                pltpu.VMEM((heads, rowtok, WIDTH), F32),
                pltpu.VMEM((heads, tiles, 8, WIDTH), F32),
                pltpu.VMEM((heads, rowtok, WIDTH), F32),
                pltpu.VMEM((heads, tiles, WIDTH, WIDTH), F32),
                pltpu.VMEM((heads, tiles, WIDTH, WIDTH), F32),
                pltpu.VMEM((group, rowtok, 2 * rowtok), BF16),
                pltpu.VMEM((heads, slots, 2 * rowtok), BF16),
                dma((12,)),
                dma((nz, len(parcels))),
                dma((nz, len(parcels))),
                dma((nz,)),
                dma((nz,)),
                dma((RUNS, heads)),
                dma((RUNS, heads)),
                pltpu.SemaphoreType.REGULAR,
                pltpu.SemaphoreType.REGULAR,
            ],
            compiler_params=pltpu.CompilerParams(
                collective_id=0, has_side_effects=True, vmem_limit_bytes=60 * 1024 * 1024
            ),
            name="delta",
        )(
            queries, keys, values, log_decay, beta_logit.T, block_owner, block_start,
            gain.reshape(1, -1),
        )

    return jax.shard_map(
        local,
        mesh=mesh,
        in_specs=(P(("doc", "head"), None),) * 5 + (P(), P(), P("head")),
        out_specs=P("doc", "head"),
        check_vma=False,
    )
```

```python
import functools

import jax
import jax.numpy as jnp
from jax import lax
from jax.experimental import pallas as pl
from jax.experimental.pallas import tpu as pltpu
from jax.sharding import PartitionSpec as P

WIDTH = 128
BLOCK = 16
TILE = 128
RUNS = 4
BASE = 16
AHEAD = 3
LOW_HOME, HIGH_HOME = 1, 2
AT_ONCE = {True: (), False: ()}
AFTER_ONE = {True: (1, 2, 3), False: (1, 2, 3)}
AFTER_TWO = {True: (4,), False: (4,)}
AFTER = {True: ((), (), (), (), ()), False: ((), (), (), (), ())}
CLOSE_AT = {True: 2, False: 2}

MESH = pl.DeviceIdType.MESH
F32 = jnp.float32
BF16 = jnp.bfloat16
NN = (((1,), (0,)), ((), ()))
NT = (((1,), (1,)), ((), ()))
TN = (((0,), (0,)), ((), ()))


def split(x):
    high = x.astype(BF16)
    return high, (x - high.astype(F32)).astype(BF16)


def bdot(a, b, dims=NN):
    return lax.dot_general(a, b, dims, preferred_element_type=F32)


def dot3(a, b, dims=NN):
    a_high, a_low = split(a) if not isinstance(a, tuple) else a
    b_high, b_low = split(b) if not isinstance(b, tuple) else b
    ca, cb = dims[0][0][0], dims[0][1][0]
    left = jnp.concatenate([a_high, a_low], axis=ca)
    free = 1 - cb
    top = jnp.concatenate([b_high, b_low], axis=free)
    bottom = jnp.concatenate([b_high, jnp.zeros_like(b_low)], axis=free)
    both = bdot(left, jnp.concatenate([top, bottom], axis=cb), dims)
    width = both.shape[1] // 2
    return both[:, :width] + both[:, width:]


def lane_iota(shape):
    return lax.broadcasted_iota(jnp.int32, shape, 1)


def row_iota(shape):
    return lax.broadcasted_iota(jnp.int32, shape, 0)


def neumann(neg, order, eye):
    power = [dot3(n, n) for n in neg]
    total = [eye + n for n in neg]
    size = 2
    while size < order:
        if size * 2 >= order:
            total = [x + dot3(x, p) for x, p in zip(total, power)]
        else:
            both = [dot3(jnp.concatenate([x, p], axis=0), p) for x, p in zip(total, power)]
            total = [x + b[:TILE] for x, b in zip(total, both)]
            power = [b[TILE:] for b in both]
        size *= 2
    return total


def inverses(mats):
    shape = (TILE, TILE)
    row, col = row_iota(shape), lane_iota(shape)
    eye = (row == col).astype(F32)
    diag = row // BASE == col // BASE
    inner = neumann([jnp.where(diag, -a, 0.0) for a in mats], BASE, eye)
    parts = [split(x) for x in inner]
    outer = [-dot3(p, jnp.where(diag, 0.0, a)) for p, a in zip(parts, mats)]
    return [dot3(y, p) for y, p in zip(neumann(outer, TILE // BASE, eye), parts)]


def rows_of(steps, body):
    if steps <= 4:
        for step in range(steps):
            body(step)
    else:
        lax.fori_loop(0, steps, lambda step, carry: (body(step), carry)[1], 0)


def kernel(
    nz, nd, parcels, shared, q_ref, k_ref, v_ref, g_ref, b_ref, owner_in, start_in, gain_in, out_ref,
    buf, held, bbuf, owner_ref, start_ref, gain_ref, betas, brows, place, stage, segcol, masks,
    growth, keyinv, keystate, halves, weights, ends, carries, mats, placed,
    local_sem, send_sem, recv_sem, bsend_sem, brecv_sem, osend_sem, orecv_sem,
    row_sem, all_sem, *rest,
):
    me = lax.axis_index("head")
    doc = lax.axis_index("doc")
    _, rowtok, columns = buf.shape
    heads = columns // WIDTH
    tok = q_ref.shape[0]
    nblk = rowtok // BLOCK
    cap = 2 * nblk // RUNS
    capt = cap * BLOCK
    tiles = rowtok // TILE
    slots = RUNS * capt
    shape = (TILE, TILE)
    refs = (k_ref, g_ref, q_ref, v_ref)

    def greet(semaphore):
        for step in peers:
            pl.semaphore_signal(
                semaphore, inc=1, device_id={"doc": lax.rem(doc + step, nd)}, device_id_type=MESH
            )

    barrier = pltpu.get_barrier_semaphore()
    count = 0
    for step in range(1, nz):
        pl.semaphore_signal(
            barrier, inc=1, device_id={"head": lax.rem(me + step, nz)}, device_id_type=MESH
        )
        count += 1
    peers = sorted({s % nd for s in range(1, RUNS)} | {(-s) % nd for s in range(1, RUNS)})
    leader = me == 0

    @pl.when(leader)
    def _():
        greet(barrier)


    mine = pl.ds(pl.multiple_of(me * tok, tok), tok)
    own = pl.ds(pl.multiple_of(me * columns, columns), columns)
    fetch = [pltpu.make_async_copy(refs[w], held.at[w], local_sem.at[w]) for w in range(4)]
    small = [
        pltpu.make_async_copy(source, target, local_sem.at[4 + index])
        for index, (source, target) in enumerate(
            [(owner_in, owner_ref), (start_in, start_ref), (gain_in, gain_ref), (b_ref, bbuf.at[me])]
        )
    ]
    keep = [
        pltpu.make_async_copy(refs[w].at[:, own], buf.at[w, mine, :], local_sem.at[8 + w])
        for w in range(4)
    ]
    half = nz // 2
    below = me < half
    base = jnp.where(below, 0, half)
    mate = jnp.where(below, me + half, me - half)
    if shared:
        (
            fbuf, fgain, codes, coded, sizes, sized, give, got, near, reads, frees,
            fsend, frecv, xsend, xrecv,
        ) = rest
        seat = pl.ds(pl.multiple_of((me - base) * tok, tok), tok)
        theirs = pl.ds(pl.multiple_of(mate * columns, columns), fbuf.shape[2])
        keep += [
            pltpu.make_async_copy(refs[w].at[:, theirs], fbuf.at[w, seat, :], local_sem.at[12 + w])
            for w in range(4)
        ]
    for copy in fetch + small + keep:
        copy.start()
    for copy in small:
        copy.wait()
    here = row_iota((nd, nblk)) == doc
    owner = jnp.sum(jnp.where(here, owner_ref[...], 0), axis=0, keepdims=True)
    start = jnp.sum(jnp.where(here, start_ref[...], 0), axis=0, keepdims=True)
    eye_b = row_iota((nblk, nblk)) == lane_iota((nblk, nblk))
    owner_col = jnp.sum(jnp.where(eye_b, owner, 0), axis=1, keepdims=True)
    earlier = row_iota((nblk, nblk)) < lane_iota((nblk, nblk))
    rank = jnp.sum(jnp.where(earlier & (owner_col == owner), 1, 0), axis=0, keepdims=True)
    ahead = owner - doc
    ahead = jnp.where(ahead < 0, ahead + nd, ahead)
    slot = (ahead * cap + rank).astype(F32).astype(BF16)
    token_block = lane_iota((nblk, rowtok)) // BLOCK
    expand = (row_iota((nblk, rowtok)) == token_block).astype(F32).astype(BF16)
    slot_tok = bdot(slot, expand).astype(jnp.int32) * BLOCK + lane_iota((1, rowtok)) % BLOCK
    place[...] = (row_iota((slots, rowtok)) == slot_tok).astype(F32).astype(BF16)
    upto = (row_iota((nblk, rowtok)) <= token_block).astype(F32).astype(BF16)
    seg_row = bdot(start.astype(F32).astype(BF16), upto)
    seg_col = jnp.sum(
        jnp.where(
            lane_iota((rowtok, nblk)) <= row_iota((rowtok, nblk)) // BLOCK, start.astype(F32), 0.0
        ),
        axis=1,
        keepdims=True,
    )
    segcol[...] = jnp.broadcast_to(seg_col, (rowtok, WIDTH))
    for tile in range(tiles):
        lo = tile * TILE
        same = seg_col[lo : lo + TILE] == seg_row[:, lo : lo + TILE]
        masks[tile, 0] = (same & (row_iota(shape) > lane_iota(shape))).astype(F32)
        masks[tile, 1] = (same & (row_iota(shape) >= lane_iota(shape))).astype(F32)
    for tile in range(tiles - 1):
        lo = tile * TILE
        for part in range(2):
            wide = pl.ds(part * rowtok + lo + TILE, rowtok - lo - TILE)
            mats[:, lo : lo + TILE, wide] = jnp.zeros(
                (mats.shape[0], TILE, rowtok - lo - TILE), BF16
            )

    for copy in fetch:
        copy.wait()

    @pl.when(leader)
    def _():
        pl.semaphore_wait(barrier, count + len(peers))
        greet(row_sem)

    @pl.when(me != 0)
    def _():
        pl.semaphore_wait(barrier, count)

    def incoming(step, parcel):
        (first, last), (low, high) = parcels[parcel]
        partner = lax.rem(me + step, nz)
        begin = pl.multiple_of(partner * columns + low * WIDTH, WIDTH)
        return pltpu.make_async_remote_copy(
            src_ref=held.at[first:last, :, pl.ds(begin, (high - low) * WIDTH)],
            dst_ref=buf.at[first:last, mine, low * WIDTH : high * WIDTH],
            send_sem=send_sem.at[step, parcel],
            recv_sem=recv_sem.at[step, parcel],
            device_id={"head": partner},
            device_id_type=MESH,
        )

    def incoming_beta(step):
        return pltpu.make_async_remote_copy(
            src_ref=b_ref,
            dst_ref=bbuf.at[me],
            send_sem=bsend_sem.at[step],
            recv_sem=brecv_sem.at[step],
            device_id={"head": lax.rem(me + step, nz)},
            device_id_type=MESH,
        )

    def outgoing(run, head):
        rows = pl.ds(run * capt, capt)
        return pltpu.make_async_remote_copy(
            src_ref=stage.at[head, rows, :],
            dst_ref=out_ref.at[rows, pl.ds(pl.multiple_of(head * WIDTH, WIDTH), WIDTH)],
            send_sem=osend_sem.at[run, head],
            recv_sem=orecv_sem.at[run, head],
            device_id={"doc": lax.rem(doc + run, nd)},
            device_id_type=MESH,
        )

    steps = sorted(range(1, nz), key=lambda s: (-min(s, nz - s), s))
    cross = list(range(half, nz))
    beside = list(range(1, half))
    kinds = {True: LOW_HOME, False: HIGH_HOME}

    def person(step):
        if step < half:
            return base + lax.rem(me - base + step, half)
        return half - base + lax.rem(me - base + step - half, half)

    def parcel_to(low, step, index):
        (first, last), (begin, end) = homes(heads, kinds[low])[index]
        partner = person(step)
        column = pl.multiple_of(partner * columns + begin * WIDTH, WIDTH)
        return pltpu.make_async_remote_copy(
            src_ref=held.at[first:last, :, pl.ds(column, (end - begin) * WIDTH)],
            dst_ref=buf.at[first:last, mine, begin * WIDTH : end * WIDTH],
            send_sem=send_sem.at[step, index],
            recv_sem=recv_sem.at[step, index],
            device_id={"head": partner},
            device_id_type=MESH,
        )

    def early_own(low, step):
        wide = kinds[low] * WIDTH
        partner = person(step)
        return pltpu.make_async_remote_copy(
            src_ref=held.at[:, :, pl.ds(pl.multiple_of(partner * columns, WIDTH), wide)],
            dst_ref=buf.at[:, mine, 0:wide],
            send_sem=fsend.at[step, 0],
            recv_sem=frecv.at[step, 0],
            device_id={"head": partner},
            device_id_type=MESH,
        )

    def early_other(low, step):
        wide = kinds[not low] * WIDTH
        partner = person(step)
        origin = half - base + partner - base
        return pltpu.make_async_remote_copy(
            src_ref=held.at[:, :, pl.ds(pl.multiple_of(origin * columns, WIDTH), wide)],
            dst_ref=fbuf.at[:, seat, 0:wide],
            send_sem=fsend.at[step, 1],
            recv_sem=frecv.at[step, 1],
            device_id={"head": partner},
            device_id_type=MESH,
        )

    def to_mate(source, target, index):
        return pltpu.make_async_remote_copy(
            src_ref=source,
            dst_ref=target,
            send_sem=xsend.at[index],
            recv_sem=xrecv.at[index],
            device_id={"head": mate},
            device_id_type=MESH,
        )

    def gain_over():
        return to_mate(gain_ref, fgain, 0)

    def states_over(part):
        some = pl.ds(0, LOW_HOME) if part == 0 else pl.ds(LOW_HOME, HIGH_HOME)
        return [
            to_mate(sizes.at[some], sized.at[some], 4 + part),
            to_mate(codes.at[some], coded.at[some], 1 + part),
        ]

    def half_over(low):
        count = kinds[not low]
        return to_mate(give.at[0:count], got.at[0:count], 3)

    def send_parcels(low, index):
        for step in cross:
            parcel_to(not low, step, index).start()
        for step in beside:
            parcel_to(low, step, index).start()

    for step in steps:
        incoming_beta(step).start()
    if shared:

        def begin_sends(low):
            for step in beside:
                (early_own if low else early_other)(low, step).start()
            for step in cross:
                parcel_to(not low, step, 0).start()
            for step in beside:
                (early_other if low else early_own)(low, step).start()
            for step in beside:
                parcel_to(low, step, 0).start()
            for index in AT_ONCE[low]:
                send_parcels(low, index)

        @pl.when(below)
        def _():
            begin_sends(True)

        @pl.when(jnp.logical_not(below))
        def _():
            begin_sends(False)

    else:
        for parcel in range(min(AHEAD, len(parcels))):
            for step in steps:
                incoming(step, parcel).start()

    if shared:
        gain_over().start()
    for step in range(1, nz):
        incoming_beta(step).wait_recv()

    eye_tok = (row_iota((tok, tok)) == lane_iota((tok, tok))).astype(F32).astype(BF16)
    flat = jnp.zeros((bbuf.shape[1], rowtok), F32)
    for step in range(nz):
        turned = bdot(eye_tok, bbuf[step], NT)
        betas[step * tok : (step + 1) * tok, :] = jax.nn.sigmoid(turned)
        shift = row_iota((tok, rowtok)) + step * tok == lane_iota((tok, rowtok))
        flat = flat + bdot(bbuf[step], shift.astype(F32).astype(BF16))
    brows[...] = jax.nn.sigmoid(flat)

    for copy in keep:
        copy.wait()

    @pl.when(leader)
    def _():
        pl.semaphore_wait(row_sem, len(peers))
        for step in range(1, nz):
            pl.semaphore_signal(
                all_sem, inc=1, device_id={"head": lax.rem(me + step, nz)}, device_id_type=MESH
            )

    @pl.when(me != 0)
    def _():
        pl.semaphore_wait(all_sem, 1)

    def arrive(parcel):
        for step in range(1, nz):
            incoming(step, parcel).wait_recv()

    def beta_of(head):
        values = betas[...]
        mine_here = lane_iota(values.shape) == me * heads + head
        return jnp.sum(jnp.where(mine_here, values, 0.0), axis=1, keepdims=True)

    def before(tile):
        return segcol[tile * TILE - 1 : tile * TILE, :]

    def final(tile):
        return segcol[(tile + 1) * TILE - 1 : (tile + 1) * TILE, :]

    def lanes(head):
        return pl.ds(head * WIDTH, WIDTH)

    def keys_part(members):
        lower = (row_iota(shape) >= lane_iota(shape)).astype(F32).astype(BF16)
        where, amats, tails = [], [], []
        for head in members:
            beta = beta_of(head)
            for tile in range(tiles):
                rows = pl.ds(tile * TILE, TILE)
                seg = segcol[rows, :]
                key = buf[0, rows, lanes(head)].astype(F32)
                key = key * lax.rsqrt(jnp.sum(key * key, axis=-1, keepdims=True) + 1e-06)
                cumul = bdot(lower, buf[1, rows, lanes(head)])
                half = 0.5 * cumul[TILE - 1 :, :]
                grow = jnp.exp(cumul - half)
                middle = jnp.exp(half)
                kg, ki = key * grow, key * jnp.exp(half - cumul)
                amat = dot3(kg, ki, NT)
                amat = jnp.where(masks[tile, 0] > 0.0, amat, 0.0)
                amats.append(amat * beta[tile * TILE : (tile + 1) * TILE])
                where.append((head, tile, rows))
                growth[head, rows, :] = grow
                keyinv[head, rows, :] = ki
                halves[head, tile] = jnp.broadcast_to(middle, (8, WIDTH))
                if tile > 0:
                    keystate[head, rows, :] = kg * ((seg == before(tile)).astype(F32) * middle)
                tails.append(ki * ((seg == final(tile)).astype(F32) * middle))
        solved = []
        for (head, tile, rows), inv in zip(where, inverses(amats)):
            row = brows[pl.ds(me * heads + head, 1), :]
            scaled = inv * row[:, tile * TILE : (tile + 1) * TILE]
            weights[head, rows, :] = scaled
            solved.append(scaled)
        made = [
            dot3(t, w, TN) if tile < tiles - 1 else None
            for (head, tile, rows), t, w in zip(where, tails, solved)
        ]
        for (head, tile, rows), end in zip(where, made):
            if tile < tiles - 1:
                ends[head, tile] = end
                if tile > 0:
                    middle = halves[head, tile, 0:1, :]
                    scale = middle * middle * (final(tile) == before(tile)).astype(F32)
                    eye = row_iota(shape) == lane_iota(shape)
                    carries[head, tile] = jnp.where(eye, scale, 0.0) - dot3(
                        end, keystate[head, rows, :]
                    )

    def store(index, tile, source, block):
        high, low = split(block)
        rows = pl.ds(tile * TILE, TILE)
        mats[index, rows, pl.ds(source * TILE, TILE)] = high
        mats[index, rows, pl.ds(rowtok + source * TILE, TILE)] = low

    def queries_part(members):
        where, grown, scores = [], [], []
        for index, head in enumerate(members):
            for tile in range(tiles):
                rows = pl.ds(tile * TILE, TILE)
                query = buf[2, rows, lanes(head)].astype(F32)
                query = (
                    query
                    * lax.rsqrt(jnp.sum(query * query, axis=-1, keepdims=True) + 1e-06)
                    * WIDTH ** (-0.5)
                )
                qg = query * growth[head, rows, :]
                score = dot3(qg, keyinv[head, rows, :], NT)
                scores.append(jnp.where(masks[tile, 1] > 0.0, score, 0.0))
                grown.append(qg)
                where.append((index, head, tile, rows))
        inner = [
            dot3(score, weights[head, rows, :])
            for (index, head, tile, rows), score in zip(where, scores)
        ]
        reads = []
        for (index, head, tile, rows), block, qg in zip(where, inner, grown):
            store(index, tile, tile, block)
            if tile > 0:
                first = (segcol[rows, :] == before(tile)).astype(F32) * halves[head, tile, 0:1, :]
                reads.append(qg * first - dot3(block, keystate[head, rows, :]))
            else:
                reads.append(None)
        for index, head in enumerate(members):
            for source in range(tiles - 1):
                state = ends[head, source]
                for tile in range(source + 1, tiles):
                    parts = split(state)
                    store(index, tile, source, dot3(reads[index * tiles + tile], parts))
                    if tile < tiles - 1:
                        state = dot3(carries[head, tile], parts)
        for index, head in enumerate(members):

            def move(step):
                rows = pl.ds(pl.multiple_of(step * TILE, TILE), TILE)
                placed[head, rows, :] = bdot(place[rows, :], mats[index]).astype(BF16)

            rows_of(slots // TILE, move)

    def values_part(head):
        value = buf[3, :, lanes(head)]
        value = jnp.concatenate([value, value], axis=0)
        gain = gain_ref[:, lanes(head)]
        for run in list(range(2, RUNS)) + [1, 0]:
            rows = pl.ds(run * capt, capt)
            result = bdot(placed[head, rows, :], value)
            norm = lax.rsqrt(jnp.mean(result * result, axis=-1, keepdims=True) + 1e-05)
            result = (result * norm * gain).astype(BF16)
            if run == 0:
                out_ref[rows, lanes(head)] = result
            else:
                stage[head, rows, :] = result
                outgoing(run, head).start()

    def of_value(matrix, value):
        high, low = split(matrix)
        return bdot(
            jnp.concatenate([high, low], axis=1), jnp.concatenate([value, value], axis=0)
        )

    def normed(result, gain):
        norm = lax.rsqrt(jnp.mean(result * result, axis=-1, keepdims=True) + 1e-05)
        return (result * norm * gain).astype(BF16)

    def tile_part(tile, items):
        rows = slice(tile * TILE, (tile + 1) * TILE)
        lower = (row_iota(shape) >= lane_iota(shape)).astype(F32).astype(BF16)
        seg = segcol[rows, :]
        kept, amats = [], []
        for load, place_of in items:
            values = betas[rows, :]
            beta = jnp.sum(
                jnp.where(lane_iota(values.shape) == place_of, values, 0.0), axis=1, keepdims=True
            )
            key = load(0).astype(F32)
            key = key * lax.rsqrt(jnp.sum(key * key, axis=-1, keepdims=True) + 1e-06)
            cumul = bdot(lower, load(1))
            mid = 0.5 * cumul[TILE - 1 :, :]
            grow = jnp.exp(cumul - mid)
            middle = jnp.exp(mid)
            kg, ki = key * grow, key * jnp.exp(mid - cumul)
            amat = jnp.where(masks[tile, 0] > 0.0, dot3(kg, ki, NT), 0.0)
            amats.append(amat * beta)
            query = load(2).astype(F32)
            query = (
                query
                * lax.rsqrt(jnp.sum(query * query, axis=-1, keepdims=True) + 1e-06)
                * WIDTH ** (-0.5)
            )
            qg = query * grow
            score = jnp.where(masks[tile, 1] > 0.0, dot3(qg, ki, NT), 0.0)
            kept.append((kg, ki, middle, qg, score))
        solved = [
            inv * brows[pl.ds(place_of, 1), :][:, rows]
            for (load, place_of), inv in zip(items, inverses(amats))
        ]
        inner = [dot3(score, w) for (kg, ki, middle, qg, score), w in zip(kept, solved)]
        if tile == 0:
            outer = [
                dot3(ki * ((seg == final(0)).astype(F32) * middle), w, TN)
                for (kg, ki, middle, qg, score), w in zip(kept, solved)
            ]
        else:
            outer = []
            for (kg, ki, middle, qg, score), block in zip(kept, inner):
                first = (seg == before(tile)).astype(F32) * middle
                outer.append(qg * first - dot3(block, kg * first))
        return inner, outer

    def put(head, both):
        full = bdot(place[...], both).astype(BF16)
        for run in list(range(2, RUNS)) + [1, 0]:
            rows = pl.ds(run * capt, capt)
            piece = full[run * capt : (run + 1) * capt]
            if run == 0:
                out_ref[rows, lanes(head)] = piece
            else:
                stage[head, rows, :] = piece
                outgoing(run, head).start()

    def role(low):
        home, other = kinds[low], kinds[not low]
        tile = 0 if low else 1
        area = slice(tile * TILE, (tile + 1) * TILE)

        def from_own(head):
            return (lambda w: buf[w, area, lanes(head)]), me * heads + head

        def from_other(head):
            return (lambda w: fbuf[w, :, lanes(head)]), mate * heads + head

        def settle(index):
            for step in cross + beside:
                parcel_to(low, step, index).wait_recv()

        def meet(part):
            for copy in states_over(part):
                copy.wait_recv()
            for slot in range(other) if part == 0 else range(other, home + other):
                result = (
                    dot3(reads[slot], coded[slot].astype(jnp.int32).astype(F32))
                    * sized[slot, 0:1, :]
                    + frees[slot]
                )
                if part == 0:
                    give[slot] = normed(result, fgain[:, lanes(slot)])
                else:
                    near[slot - other] = normed(result, gain_ref[:, lanes(slot - other)])
            if part == 0:
                half_over(low).start()

        def close():
            half_over(not low).wait_recv()
            for head in range(home):
                ordered = [near[head], got[head]] if low else [got[head], near[head]]
                put(head, jnp.concatenate(ordered, axis=0))

        def early(own, step):
            return early_own(low, step) if own else early_other(low, step)

        def phase(part):
            own = low == (part == 0)
            if own:
                items = [from_own(head) for head in range(home)]
            else:
                items = [from_other(head) for head in range(other)]
            shift = 0 if part == 0 else LOW_HOME
            for step in beside:
                early(own, step).wait_recv()
            inner, outer = tile_part(tile, items)
            values = [load(3) for load, place_of in items]
            if low:
                for slot, (block, value) in enumerate(zip(outer, values)):
                    state = of_value(block, value)
                    most = jnp.maximum(jnp.max(jnp.abs(state), axis=0, keepdims=True), 1e-30)
                    code = jnp.round(state * (32767.0 / most)).astype(jnp.int32)
                    codes[shift + slot] = code.astype(jnp.int16)
                    sizes[shift + slot] = jnp.broadcast_to(most * (1.0 / 32767.0), (8, WIDTH))
                for copy in states_over(part):
                    copy.start()
            for slot, (block, value) in enumerate(zip(inner, values)):
                result = of_value(block, value)
                if not low:
                    reads[shift + slot] = outer[slot]
                    frees[shift + slot] = result
                elif own:
                    near[slot] = normed(result, gain_ref[:, lanes(slot)])
                else:
                    give[slot] = normed(result, fgain[:, lanes(slot)])
            if low and not own:
                half_over(low).start()

        phase(0)
        for index in AFTER_ONE[low]:
            send_parcels(low, index)
        gain_over().wait_recv()
        phase(1)
        if not low:
            meet(0)
        for index in AFTER_TWO[low]:
            send_parcels(low, index)

        plan = homes(heads, home)
        for index, ((first, last), (begin, end)) in enumerate(plan):
            settle(index)
            for later in AFTER[low][index]:
                send_parcels(low, later)
            if first == 0:
                keys_part(list(range(begin, end)))
            elif first == 2:
                queries_part(list(range(begin, end)))
            else:
                for head in range(begin, end):
                    values_part(head)
            if index == CLOSE_AT[low]:
                if not low:
                    meet(1)
                close()
        for index in range(len(plan)):
            for step in beside:
                parcel_to(low, step, index).wait_send()
            for step in cross:
                parcel_to(not low, step, index).wait_send()
        for step in beside:
            early_own(low, step).wait_send()
            early_other(low, step).wait_send()
        if low:
            for copy in states_over(0) + states_over(1):
                copy.wait_send()
        gain_over().wait_send()
        half_over(low).wait_send()

    if shared:

        @pl.when(below)
        def _():
            role(True)

        @pl.when(jnp.logical_not(below))
        def _():
            role(False)

    else:
        group = mats.shape[0]
        for parcel, ((first, last), (low, high)) in enumerate(parcels):
            arrive(parcel)
            if parcel + AHEAD < len(parcels):
                for step in steps:
                    incoming(step, parcel + AHEAD).start()
            for begin in range(low, high, group):
                members = list(range(begin, min(begin + group, high)))
                if first == 0:
                    keys_part(members)
                if first <= 2 < last:
                    queries_part(members)
            if last == 4:
                for head in range(low, high):
                    values_part(head)

    for step in range(1, nz):
        incoming_beta(step).wait_send()
        for parcel in range(0 if shared else len(parcels)):
            incoming(step, parcel).wait_send()
    for head in range(heads):
        for run in range(1, RUNS):
            outgoing(run, head).wait()


def homes(heads, begin):
    early = heads - 1
    return [
        ((0, 2), (begin, heads)),
        ((2, 3), (begin, early)),
        ((3, 4), (begin, early)),
        ((2, 3), (early, heads)),
        ((3, 4), (early, heads)),
    ]


def parcels_of(heads):
    group = 2 if heads % 2 == 0 else 1
    pairs = [(low, low + group) for low in range(0, heads, group)]
    return (
        [((0, 2), pair) for pair in pairs]
        + [part for pair in pairs[:-1] for part in (((2, 3), pair), ((3, 4), pair))]
        + [((2, 3), pairs[-1])]
        + [((3, 4), (head, head + 1)) for head in range(*pairs[-1])]
    )


def solution(mesh):
    nz, nd = mesh.shape["head"], mesh.shape["doc"]

    def local(queries, keys, values, log_decay, beta_logit, block_owner, block_start, gain):
        tok, channels = queries.shape
        heads = channels // WIDTH // nz
        rowtok = tok * nz
        slots = 2 * rowtok
        tiles = rowtok // TILE
        shared = nz % 2 == 0 and tiles == 2 and tok * (nz // 2) == TILE and heads >= HIGH_HOME + 2
        group = heads - LOW_HOME if shared else 2 if heads % 2 == 0 else 1
        parcels = parcels_of(heads)
        most, both = max(LOW_HOME, HIGH_HOME), LOW_HOME + HIGH_HOME
        anywhere = pl.BlockSpec(memory_space=pl.ANY)
        dma = pltpu.SemaphoreType.DMA
        return pl.pallas_call(
            functools.partial(kernel, nz, nd, parcels, shared),
            out_shape=pltpu.VMEM((slots, heads * WIDTH), BF16),
            in_specs=[anywhere] * 8,
            out_specs=pl.BlockSpec(memory_space=pltpu.VMEM),
            scratch_shapes=[
                pltpu.VMEM((4, rowtok, heads * WIDTH), BF16),
                pltpu.VMEM((4, tok, channels), BF16),
                pltpu.VMEM((nz, beta_logit.shape[1], tok), BF16),
                pltpu.VMEM(block_owner.shape, jnp.int32),
                pltpu.VMEM(block_start.shape, jnp.int32),
                pltpu.VMEM((1, heads * WIDTH), F32),
                pltpu.VMEM((rowtok, beta_logit.shape[1]), F32),
                pltpu.VMEM((beta_logit.shape[1], rowtok), F32),
                pltpu.VMEM((slots, rowtok), BF16),
                pltpu.VMEM((heads, slots, WIDTH), BF16),
                pltpu.VMEM((rowtok, WIDTH), F32),
                pltpu.VMEM((tiles, 2, TILE, TILE), F32),
                pltpu.VMEM((heads, rowtok, WIDTH), F32),
                pltpu.VMEM((heads, rowtok, WIDTH), F32),
                pltpu.VMEM((heads, rowtok, WIDTH), F32),
                pltpu.VMEM((heads, tiles, 8, WIDTH), F32),
                pltpu.VMEM((heads, rowtok, WIDTH), F32),
                pltpu.VMEM((heads, tiles, WIDTH, WIDTH), F32),
                pltpu.VMEM((heads, tiles, WIDTH, WIDTH), F32),
                pltpu.VMEM((group, rowtok, 2 * rowtok), BF16),
                pltpu.VMEM((heads, slots, 2 * rowtok), BF16),
                dma((16,)),
                dma((nz, len(parcels))),
                dma((nz, len(parcels))),
                dma((nz,)),
                dma((nz,)),
                dma((RUNS, heads)),
                dma((RUNS, heads)),
                pltpu.SemaphoreType.REGULAR,
                pltpu.SemaphoreType.REGULAR,
            ]
            + [
                pltpu.VMEM((4, TILE, most * WIDTH), BF16),
                pltpu.VMEM((1, heads * WIDTH), F32),
                pltpu.VMEM((both, TILE, WIDTH), jnp.int16),
                pltpu.VMEM((both, TILE, WIDTH), jnp.int16),
                pltpu.VMEM((both, 8, WIDTH), F32),
                pltpu.VMEM((both, 8, WIDTH), F32),
                pltpu.VMEM((most, TILE, WIDTH), BF16),
                pltpu.VMEM((most, TILE, WIDTH), BF16),
                pltpu.VMEM((most, TILE, WIDTH), BF16),
                pltpu.VMEM((both, TILE, WIDTH), F32),
                pltpu.VMEM((both, TILE, WIDTH), F32),
                dma((nz, 2)),
                dma((nz, 2)),
                dma((6,)),
                dma((6,)),
            ]
            * shared,
            compiler_params=pltpu.CompilerParams(
                collective_id=0, has_side_effects=True, vmem_limit_bytes=60 * 1024 * 1024
            ),
            name="delta",
        )(
            queries, keys, values, log_decay, beta_logit.T, block_owner, block_start,
            gain.reshape(1, -1),
        )

    return jax.shard_map(
        local,
        mesh=mesh,
        in_specs=(P(("doc", "head"), None),) * 5 + (P(), P(), P("head")),
        out_specs=P("doc", "head"),
        check_vma=False,
    )
```

```python
import functools

import jax
import jax.numpy as jnp
from jax import lax
from jax.experimental import pallas as pl
from jax.experimental.pallas import tpu as pltpu
from jax.sharding import PartitionSpec as P

WIDTH = 128
BLOCK = 16
TILE = 128
RUNS = 4
BASE = 16
AHEAD = 3
LOW_HOME, HIGH_HOME = 1, 2
AT_ONCE = {True: (), False: ()}
AFTER_ONE = {True: (1, 2, 3), False: (1, 2)}
AFTER_TWO = {True: (4,), False: (3, 4)}
AFTER = {True: ((), (), (), (), ()), False: ((), (), (), (), ())}
CLOSE_AT = {True: 1, False: 2}

MESH = pl.DeviceIdType.MESH
F32 = jnp.float32
BF16 = jnp.bfloat16
NN = (((1,), (0,)), ((), ()))
NT = (((1,), (1,)), ((), ()))
TN = (((0,), (0,)), ((), ()))


def split(x):
    high = x.astype(BF16)
    return high, (x - high.astype(F32)).astype(BF16)


def bdot(a, b, dims=NN):
    return lax.dot_general(a, b, dims, preferred_element_type=F32)


def dot3(a, b, dims=NN):
    a_high, a_low = split(a) if not isinstance(a, tuple) else a
    b_high, b_low = split(b) if not isinstance(b, tuple) else b
    ca, cb = dims[0][0][0], dims[0][1][0]
    left = jnp.concatenate([a_high, a_low], axis=ca)
    free = 1 - cb
    top = jnp.concatenate([b_high, b_low], axis=free)
    bottom = jnp.concatenate([b_high, jnp.zeros_like(b_low)], axis=free)
    both = bdot(left, jnp.concatenate([top, bottom], axis=cb), dims)
    width = both.shape[1] // 2
    return both[:, :width] + both[:, width:]


def lane_iota(shape):
    return lax.broadcasted_iota(jnp.int32, shape, 1)


def row_iota(shape):
    return lax.broadcasted_iota(jnp.int32, shape, 0)


def neumann(neg, order, eye):
    power = [dot3(n, n) for n in neg]
    total = [eye + n for n in neg]
    size = 2
    while size < order:
        if size * 2 >= order:
            total = [x + dot3(x, p) for x, p in zip(total, power)]
        else:
            both = [dot3(jnp.concatenate([x, p], axis=0), p) for x, p in zip(total, power)]
            total = [x + b[:TILE] for x, b in zip(total, both)]
            power = [b[TILE:] for b in both]
        size *= 2
    return total


def inverses(mats):
    shape = (TILE, TILE)
    row, col = row_iota(shape), lane_iota(shape)
    eye = (row == col).astype(F32)
    diag = row // BASE == col // BASE
    inner = neumann([jnp.where(diag, -a, 0.0) for a in mats], BASE, eye)
    parts = [split(x) for x in inner]
    outer = [-dot3(p, jnp.where(diag, 0.0, a)) for p, a in zip(parts, mats)]
    return [dot3(y, p) for y, p in zip(neumann(outer, TILE // BASE, eye), parts)]


def rows_of(steps, body):
    if steps <= 4:
        for step in range(steps):
            body(step)
    else:
        lax.fori_loop(0, steps, lambda step, carry: (body(step), carry)[1], 0)


def kernel(
    nz, nd, parcels, shared, q_ref, k_ref, v_ref, g_ref, b_ref, owner_in, start_in, gain_in, out_ref,
    buf, held, bbuf, owner_ref, start_ref, gain_ref, betas, brows, place, stage, segcol, masks,
    growth, keyinv, keystate, halves, weights, ends, carries, mats, placed,
    local_sem, send_sem, recv_sem, bsend_sem, brecv_sem, osend_sem, orecv_sem,
    row_sem, all_sem, *rest,
):
    me = lax.axis_index("head")
    doc = lax.axis_index("doc")
    _, rowtok, columns = buf.shape
    heads = columns // WIDTH
    tok = q_ref.shape[0]
    nblk = rowtok // BLOCK
    cap = 2 * nblk // RUNS
    capt = cap * BLOCK
    tiles = rowtok // TILE
    slots = RUNS * capt
    shape = (TILE, TILE)
    refs = (k_ref, g_ref, q_ref, v_ref)

    def greet(semaphore):
        for step in peers:
            pl.semaphore_signal(
                semaphore, inc=1, device_id={"doc": lax.rem(doc + step, nd)}, device_id_type=MESH
            )

    barrier = pltpu.get_barrier_semaphore()
    count = 0
    for step in range(1, nz):
        pl.semaphore_signal(
            barrier, inc=1, device_id={"head": lax.rem(me + step, nz)}, device_id_type=MESH
        )
        count += 1
    peers = sorted({s % nd for s in range(1, RUNS)} | {(-s) % nd for s in range(1, RUNS)})
    leader = me == 0

    @pl.when(leader)
    def _():
        greet(barrier)


    mine = pl.ds(pl.multiple_of(me * tok, tok), tok)
    own = pl.ds(pl.multiple_of(me * columns, columns), columns)
    fetch = [pltpu.make_async_copy(refs[w], held.at[w], local_sem.at[w]) for w in range(4)]
    small = [
        pltpu.make_async_copy(source, target, local_sem.at[4 + index])
        for index, (source, target) in enumerate(
            [(owner_in, owner_ref), (start_in, start_ref), (gain_in, gain_ref), (b_ref, bbuf.at[me])]
        )
    ]
    keep = [
        pltpu.make_async_copy(refs[w].at[:, own], buf.at[w, mine, :], local_sem.at[8 + w])
        for w in range(4)
    ]
    half = nz // 2
    below = me < half
    base = jnp.where(below, 0, half)
    mate = jnp.where(below, me + half, me - half)
    if shared:
        (
            fbuf, fgain, codes, coded, sizes, sized, give, got, near, reads, frees,
            fsend, frecv, xsend, xrecv,
        ) = rest
        seat = pl.ds(pl.multiple_of((me - base) * tok, tok), tok)
        theirs = pl.ds(pl.multiple_of(mate * columns, columns), fbuf.shape[2])
        keep += [
            pltpu.make_async_copy(refs[w].at[:, theirs], fbuf.at[w, seat, :], local_sem.at[12 + w])
            for w in range(4)
        ]
    for copy in fetch + small + keep:
        copy.start()
    for copy in small:
        copy.wait()
    here = row_iota((nd, nblk)) == doc
    owner = jnp.sum(jnp.where(here, owner_ref[...], 0), axis=0, keepdims=True)
    start = jnp.sum(jnp.where(here, start_ref[...], 0), axis=0, keepdims=True)
    eye_b = row_iota((nblk, nblk)) == lane_iota((nblk, nblk))
    owner_col = jnp.sum(jnp.where(eye_b, owner, 0), axis=1, keepdims=True)
    earlier = row_iota((nblk, nblk)) < lane_iota((nblk, nblk))
    rank = jnp.sum(jnp.where(earlier & (owner_col == owner), 1, 0), axis=0, keepdims=True)
    ahead = owner - doc
    ahead = jnp.where(ahead < 0, ahead + nd, ahead)
    slot = (ahead * cap + rank).astype(F32).astype(BF16)
    token_block = lane_iota((nblk, rowtok)) // BLOCK
    expand = (row_iota((nblk, rowtok)) == token_block).astype(F32).astype(BF16)
    slot_tok = bdot(slot, expand).astype(jnp.int32) * BLOCK + lane_iota((1, rowtok)) % BLOCK
    place[...] = (row_iota((slots, rowtok)) == slot_tok).astype(F32).astype(BF16)
    upto = (row_iota((nblk, rowtok)) <= token_block).astype(F32).astype(BF16)
    seg_row = bdot(start.astype(F32).astype(BF16), upto)
    seg_col = jnp.sum(
        jnp.where(
            lane_iota((rowtok, nblk)) <= row_iota((rowtok, nblk)) // BLOCK, start.astype(F32), 0.0
        ),
        axis=1,
        keepdims=True,
    )
    segcol[...] = jnp.broadcast_to(seg_col, (rowtok, WIDTH))
    for tile in range(tiles):
        lo = tile * TILE
        same = seg_col[lo : lo + TILE] == seg_row[:, lo : lo + TILE]
        masks[tile, 0] = (same & (row_iota(shape) > lane_iota(shape))).astype(F32)
        masks[tile, 1] = (same & (row_iota(shape) >= lane_iota(shape))).astype(F32)
    for tile in range(tiles - 1):
        lo = tile * TILE
        for part in range(2):
            wide = pl.ds(part * rowtok + lo + TILE, rowtok - lo - TILE)
            mats[:, lo : lo + TILE, wide] = jnp.zeros(
                (mats.shape[0], TILE, rowtok - lo - TILE), BF16
            )

    for copy in fetch:
        copy.wait()

    @pl.when(leader)
    def _():
        pl.semaphore_wait(barrier, count + len(peers))
        greet(row_sem)

    @pl.when(me != 0)
    def _():
        pl.semaphore_wait(barrier, count)

    def incoming(step, parcel):
        (first, last), (low, high) = parcels[parcel]
        partner = lax.rem(me + step, nz)
        begin = pl.multiple_of(partner * columns + low * WIDTH, WIDTH)
        return pltpu.make_async_remote_copy(
            src_ref=held.at[first:last, :, pl.ds(begin, (high - low) * WIDTH)],
            dst_ref=buf.at[first:last, mine, low * WIDTH : high * WIDTH],
            send_sem=send_sem.at[step, parcel],
            recv_sem=recv_sem.at[step, parcel],
            device_id={"head": partner},
            device_id_type=MESH,
        )

    def incoming_beta(step):
        return pltpu.make_async_remote_copy(
            src_ref=b_ref,
            dst_ref=bbuf.at[me],
            send_sem=bsend_sem.at[step],
            recv_sem=brecv_sem.at[step],
            device_id={"head": lax.rem(me + step, nz)},
            device_id_type=MESH,
        )

    def outgoing(run, head):
        rows = pl.ds(run * capt, capt)
        return pltpu.make_async_remote_copy(
            src_ref=stage.at[head, rows, :],
            dst_ref=out_ref.at[rows, pl.ds(pl.multiple_of(head * WIDTH, WIDTH), WIDTH)],
            send_sem=osend_sem.at[run, head],
            recv_sem=orecv_sem.at[run, head],
            device_id={"doc": lax.rem(doc + run, nd)},
            device_id_type=MESH,
        )

    steps = sorted(range(1, nz), key=lambda s: (-min(s, nz - s), s))
    cross = list(range(half, nz))
    beside = list(range(1, half))
    kinds = {True: LOW_HOME, False: HIGH_HOME}

    def person(step):
        if step < half:
            return base + lax.rem(me - base + step, half)
        return half - base + lax.rem(me - base + step - half, half)

    def parcel_to(low, step, index):
        (first, last), (begin, end) = homes(heads, kinds[low])[index]
        partner = person(step)
        column = pl.multiple_of(partner * columns + begin * WIDTH, WIDTH)
        return pltpu.make_async_remote_copy(
            src_ref=held.at[first:last, :, pl.ds(column, (end - begin) * WIDTH)],
            dst_ref=buf.at[first:last, mine, begin * WIDTH : end * WIDTH],
            send_sem=send_sem.at[step, index],
            recv_sem=recv_sem.at[step, index],
            device_id={"head": partner},
            device_id_type=MESH,
        )

    def early_own(low, step):
        wide = kinds[low] * WIDTH
        partner = person(step)
        return pltpu.make_async_remote_copy(
            src_ref=held.at[:, :, pl.ds(pl.multiple_of(partner * columns, WIDTH), wide)],
            dst_ref=buf.at[:, mine, 0:wide],
            send_sem=fsend.at[step, 0],
            recv_sem=frecv.at[step, 0],
            device_id={"head": partner},
            device_id_type=MESH,
        )

    def early_other(low, step):
        wide = kinds[not low] * WIDTH
        partner = person(step)
        origin = half - base + partner - base
        return pltpu.make_async_remote_copy(
            src_ref=held.at[:, :, pl.ds(pl.multiple_of(origin * columns, WIDTH), wide)],
            dst_ref=fbuf.at[:, seat, 0:wide],
            send_sem=fsend.at[step, 1],
            recv_sem=frecv.at[step, 1],
            device_id={"head": partner},
            device_id_type=MESH,
        )

    def to_mate(source, target, index):
        return pltpu.make_async_remote_copy(
            src_ref=source,
            dst_ref=target,
            send_sem=xsend.at[index],
            recv_sem=xrecv.at[index],
            device_id={"head": mate},
            device_id_type=MESH,
        )

    def gain_over():
        return to_mate(gain_ref, fgain, 0)

    def states_over(part):
        some = pl.ds(0, LOW_HOME) if part == 0 else pl.ds(LOW_HOME, HIGH_HOME)
        return [
            to_mate(sizes.at[some], sized.at[some], 4 + part),
            to_mate(codes.at[some], coded.at[some], 1 + part),
        ]

    def half_over(low):
        count = kinds[not low]
        return to_mate(give.at[0:count], got.at[0:count], 3)

    def send_parcels(low, index):
        for step in cross:
            parcel_to(not low, step, index).start()
        for step in beside:
            parcel_to(low, step, index).start()

    for step in steps:
        incoming_beta(step).start()
    if shared:

        def begin_sends(low):
            for step in beside:
                (early_own if low else early_other)(low, step).start()
            for step in cross:
                parcel_to(not low, step, 0).start()
            for step in beside:
                (early_other if low else early_own)(low, step).start()
            for step in beside:
                parcel_to(low, step, 0).start()
            for index in AT_ONCE[low]:
                send_parcels(low, index)

        @pl.when(below)
        def _():
            begin_sends(True)

        @pl.when(jnp.logical_not(below))
        def _():
            begin_sends(False)

    else:
        for parcel in range(min(AHEAD, len(parcels))):
            for step in steps:
                incoming(step, parcel).start()

    if shared:
        gain_over().start()
    for step in range(1, nz):
        incoming_beta(step).wait_recv()

    eye_tok = (row_iota((tok, tok)) == lane_iota((tok, tok))).astype(F32).astype(BF16)
    flat = jnp.zeros((bbuf.shape[1], rowtok), F32)
    for step in range(nz):
        turned = bdot(eye_tok, bbuf[step], NT)
        betas[step * tok : (step + 1) * tok, :] = jax.nn.sigmoid(turned)
        shift = row_iota((tok, rowtok)) + step * tok == lane_iota((tok, rowtok))
        flat = flat + bdot(bbuf[step], shift.astype(F32).astype(BF16))
    brows[...] = jax.nn.sigmoid(flat)

    for copy in keep:
        copy.wait()

    @pl.when(leader)
    def _():
        pl.semaphore_wait(row_sem, len(peers))
        for step in range(1, nz):
            pl.semaphore_signal(
                all_sem, inc=1, device_id={"head": lax.rem(me + step, nz)}, device_id_type=MESH
            )

    @pl.when(me != 0)
    def _():
        pl.semaphore_wait(all_sem, 1)

    def arrive(parcel):
        for step in range(1, nz):
            incoming(step, parcel).wait_recv()

    def beta_of(head):
        values = betas[...]
        mine_here = lane_iota(values.shape) == me * heads + head
        return jnp.sum(jnp.where(mine_here, values, 0.0), axis=1, keepdims=True)

    def before(tile):
        return segcol[tile * TILE - 1 : tile * TILE, :]

    def final(tile):
        return segcol[(tile + 1) * TILE - 1 : (tile + 1) * TILE, :]

    def lanes(head):
        return pl.ds(head * WIDTH, WIDTH)

    def keys_part(members):
        lower = (row_iota(shape) >= lane_iota(shape)).astype(F32).astype(BF16)
        where, amats, tails = [], [], []
        for head in members:
            beta = beta_of(head)
            for tile in range(tiles):
                rows = pl.ds(tile * TILE, TILE)
                seg = segcol[rows, :]
                key = buf[0, rows, lanes(head)].astype(F32)
                key = key * lax.rsqrt(jnp.sum(key * key, axis=-1, keepdims=True) + 1e-06)
                cumul = bdot(lower, buf[1, rows, lanes(head)])
                half = 0.5 * cumul[TILE - 1 :, :]
                grow = jnp.exp(cumul - half)
                middle = jnp.exp(half)
                kg, ki = key * grow, key * jnp.exp(half - cumul)
                amat = dot3(kg, ki, NT)
                amat = jnp.where(masks[tile, 0] > 0.0, amat, 0.0)
                amats.append(amat * beta[tile * TILE : (tile + 1) * TILE])
                where.append((head, tile, rows))
                growth[head, rows, :] = grow
                keyinv[head, rows, :] = ki
                halves[head, tile] = jnp.broadcast_to(middle, (8, WIDTH))
                if tile > 0:
                    keystate[head, rows, :] = kg * ((seg == before(tile)).astype(F32) * middle)
                tails.append(ki * ((seg == final(tile)).astype(F32) * middle))
        solved = []
        for (head, tile, rows), inv in zip(where, inverses(amats)):
            row = brows[pl.ds(me * heads + head, 1), :]
            scaled = inv * row[:, tile * TILE : (tile + 1) * TILE]
            weights[head, rows, :] = scaled
            solved.append(scaled)
        made = [
            dot3(t, w, TN) if tile < tiles - 1 else None
            for (head, tile, rows), t, w in zip(where, tails, solved)
        ]
        for (head, tile, rows), end in zip(where, made):
            if tile < tiles - 1:
                ends[head, tile] = end
                if tile > 0:
                    middle = halves[head, tile, 0:1, :]
                    scale = middle * middle * (final(tile) == before(tile)).astype(F32)
                    eye = row_iota(shape) == lane_iota(shape)
                    carries[head, tile] = jnp.where(eye, scale, 0.0) - dot3(
                        end, keystate[head, rows, :]
                    )

    def store(index, tile, source, block):
        high, low = split(block)
        rows = pl.ds(tile * TILE, TILE)
        mats[index, rows, pl.ds(source * TILE, TILE)] = high
        mats[index, rows, pl.ds(rowtok + source * TILE, TILE)] = low

    def queries_part(members):
        where, grown, scores = [], [], []
        for index, head in enumerate(members):
            for tile in range(tiles):
                rows = pl.ds(tile * TILE, TILE)
                query = buf[2, rows, lanes(head)].astype(F32)
                query = (
                    query
                    * lax.rsqrt(jnp.sum(query * query, axis=-1, keepdims=True) + 1e-06)
                    * WIDTH ** (-0.5)
                )
                qg = query * growth[head, rows, :]
                score = dot3(qg, keyinv[head, rows, :], NT)
                scores.append(jnp.where(masks[tile, 1] > 0.0, score, 0.0))
                grown.append(qg)
                where.append((index, head, tile, rows))
        inner = [
            dot3(score, weights[head, rows, :])
            for (index, head, tile, rows), score in zip(where, scores)
        ]
        reads = []
        for (index, head, tile, rows), block, qg in zip(where, inner, grown):
            store(index, tile, tile, block)
            if tile > 0:
                first = (segcol[rows, :] == before(tile)).astype(F32) * halves[head, tile, 0:1, :]
                reads.append(qg * first - dot3(block, keystate[head, rows, :]))
            else:
                reads.append(None)
        for index, head in enumerate(members):
            for source in range(tiles - 1):
                state = ends[head, source]
                for tile in range(source + 1, tiles):
                    parts = split(state)
                    store(index, tile, source, dot3(reads[index * tiles + tile], parts))
                    if tile < tiles - 1:
                        state = dot3(carries[head, tile], parts)
        for index, head in enumerate(members):

            def move(step):
                rows = pl.ds(pl.multiple_of(step * TILE, TILE), TILE)
                placed[head, rows, :] = bdot(place[rows, :], mats[index]).astype(BF16)

            rows_of(slots // TILE, move)

    def values_part(head):
        value = buf[3, :, lanes(head)]
        value = jnp.concatenate([value, value], axis=0)
        gain = gain_ref[:, lanes(head)]
        for run in list(range(2, RUNS)) + [1, 0]:
            rows = pl.ds(run * capt, capt)
            result = bdot(placed[head, rows, :], value)
            norm = lax.rsqrt(jnp.mean(result * result, axis=-1, keepdims=True) + 1e-05)
            result = (result * norm * gain).astype(BF16)
            if run == 0:
                out_ref[rows, lanes(head)] = result
            else:
                stage[head, rows, :] = result
                outgoing(run, head).start()

    def of_value(matrix, value):
        high, low = split(matrix)
        return bdot(
            jnp.concatenate([high, low], axis=1), jnp.concatenate([value, value], axis=0)
        )

    def normed(result, gain):
        norm = lax.rsqrt(jnp.mean(result * result, axis=-1, keepdims=True) + 1e-05)
        return (result * norm * gain).astype(BF16)

    def tile_part(tile, items):
        rows = slice(tile * TILE, (tile + 1) * TILE)
        lower = (row_iota(shape) >= lane_iota(shape)).astype(F32).astype(BF16)
        seg = segcol[rows, :]
        kept, amats = [], []
        for load, place_of in items:
            values = betas[rows, :]
            beta = jnp.sum(
                jnp.where(lane_iota(values.shape) == place_of, values, 0.0), axis=1, keepdims=True
            )
            key = load(0).astype(F32)
            key = key * lax.rsqrt(jnp.sum(key * key, axis=-1, keepdims=True) + 1e-06)
            cumul = bdot(lower, load(1))
            mid = 0.5 * cumul[TILE - 1 :, :]
            grow = jnp.exp(cumul - mid)
            middle = jnp.exp(mid)
            kg, ki = key * grow, key * jnp.exp(mid - cumul)
            amat = jnp.where(masks[tile, 0] > 0.0, dot3(kg, ki, NT), 0.0)
            amats.append(amat * beta)
            query = load(2).astype(F32)
            query = (
                query
                * lax.rsqrt(jnp.sum(query * query, axis=-1, keepdims=True) + 1e-06)
                * WIDTH ** (-0.5)
            )
            qg = query * grow
            score = jnp.where(masks[tile, 1] > 0.0, dot3(qg, ki, NT), 0.0)
            kept.append((kg, ki, middle, qg, score))
        solved = [
            inv * brows[pl.ds(place_of, 1), :][:, rows]
            for (load, place_of), inv in zip(items, inverses(amats))
        ]
        inner = [dot3(score, w) for (kg, ki, middle, qg, score), w in zip(kept, solved)]
        if tile == 0:
            outer = [
                dot3(ki * ((seg == final(0)).astype(F32) * middle), w, TN)
                for (kg, ki, middle, qg, score), w in zip(kept, solved)
            ]
        else:
            outer = []
            for (kg, ki, middle, qg, score), block in zip(kept, inner):
                first = (seg == before(tile)).astype(F32) * middle
                outer.append(qg * first - dot3(block, kg * first))
        return inner, outer

    def put(head, both):
        full = bdot(place[...], both).astype(BF16)
        for run in list(range(2, RUNS)) + [1, 0]:
            rows = pl.ds(run * capt, capt)
            piece = full[run * capt : (run + 1) * capt]
            if run == 0:
                out_ref[rows, lanes(head)] = piece
            else:
                stage[head, rows, :] = piece
                outgoing(run, head).start()

    def role(low):
        home, other = kinds[low], kinds[not low]
        tile = 0 if low else 1
        area = slice(tile * TILE, (tile + 1) * TILE)

        def from_own(head):
            return (lambda w: buf[w, area, lanes(head)]), me * heads + head

        def from_other(head):
            return (lambda w: fbuf[w, :, lanes(head)]), mate * heads + head

        def settle(index):
            for step in cross + beside:
                parcel_to(low, step, index).wait_recv()

        def meet(part):
            for copy in states_over(part):
                copy.wait_recv()
            for slot in range(other) if part == 0 else range(other, home + other):
                result = (
                    dot3(reads[slot], coded[slot].astype(jnp.int32).astype(F32))
                    * sized[slot, 0:1, :]
                    + frees[slot]
                )
                if part == 0:
                    give[slot] = normed(result, fgain[:, lanes(slot)])
                else:
                    near[slot - other] = normed(result, gain_ref[:, lanes(slot - other)])
            if part == 0:
                half_over(low).start()

        def close():
            half_over(not low).wait_recv()
            for head in range(home):
                ordered = [near[head], got[head]] if low else [got[head], near[head]]
                put(head, jnp.concatenate(ordered, axis=0))

        def early(own, step):
            return early_own(low, step) if own else early_other(low, step)

        def phase(part):
            own = low == (part == 0)
            if own:
                items = [from_own(head) for head in range(home)]
            else:
                items = [from_other(head) for head in range(other)]
            shift = 0 if part == 0 else LOW_HOME
            for step in beside:
                early(own, step).wait_recv()
            inner, outer = tile_part(tile, items)
            values = [load(3) for load, place_of in items]
            if low:
                for slot, (block, value) in enumerate(zip(outer, values)):
                    state = of_value(block, value)
                    most = jnp.maximum(jnp.max(jnp.abs(state), axis=0, keepdims=True), 1e-30)
                    code = jnp.round(state * (32767.0 / most)).astype(jnp.int32)
                    codes[shift + slot] = code.astype(jnp.int16)
                    sizes[shift + slot] = jnp.broadcast_to(most * (1.0 / 32767.0), (8, WIDTH))
                for copy in states_over(part):
                    copy.start()
            for slot, (block, value) in enumerate(zip(inner, values)):
                result = of_value(block, value)
                if not low:
                    reads[shift + slot] = outer[slot]
                    frees[shift + slot] = result
                elif own:
                    near[slot] = normed(result, gain_ref[:, lanes(slot)])
                else:
                    give[slot] = normed(result, fgain[:, lanes(slot)])
            if low and not own:
                half_over(low).start()

        phase(0)
        for index in AFTER_ONE[low]:
            send_parcels(low, index)
        gain_over().wait_recv()
        phase(1)
        if not low:
            meet(0)
        for index in AFTER_TWO[low]:
            send_parcels(low, index)

        plan = homes(heads, home)
        for index, ((first, last), (begin, end)) in enumerate(plan):
            settle(index)
            for later in AFTER[low][index]:
                send_parcels(low, later)
            if first == 0:
                keys_part(list(range(begin, end)))
            elif first == 2:
                queries_part(list(range(begin, end)))
            else:
                for head in range(begin, end):
                    values_part(head)
            if index == CLOSE_AT[low]:
                if not low:
                    meet(1)
                close()
        for index in range(len(plan)):
            for step in beside:
                parcel_to(low, step, index).wait_send()
            for step in cross:
                parcel_to(not low, step, index).wait_send()
        for step in beside:
            early_own(low, step).wait_send()
            early_other(low, step).wait_send()
        if low:
            for copy in states_over(0) + states_over(1):
                copy.wait_send()
        gain_over().wait_send()
        half_over(low).wait_send()

    if shared:

        @pl.when(below)
        def _():
            role(True)

        @pl.when(jnp.logical_not(below))
        def _():
            role(False)

    else:
        group = mats.shape[0]
        for parcel, ((first, last), (low, high)) in enumerate(parcels):
            arrive(parcel)
            if parcel + AHEAD < len(parcels):
                for step in steps:
                    incoming(step, parcel + AHEAD).start()
            for begin in range(low, high, group):
                members = list(range(begin, min(begin + group, high)))
                if first == 0:
                    keys_part(members)
                if first <= 2 < last:
                    queries_part(members)
            if last == 4:
                for head in range(low, high):
                    values_part(head)

    for step in range(1, nz):
        incoming_beta(step).wait_send()
        for parcel in range(0 if shared else len(parcels)):
            incoming(step, parcel).wait_send()
    for head in range(heads):
        for run in range(1, RUNS):
            outgoing(run, head).wait()


def homes(heads, begin):
    early = heads - 1
    return [
        ((0, 2), (begin, heads)),
        ((2, 3), (begin, early)),
        ((3, 4), (begin, early)),
        ((2, 3), (early, heads)),
        ((3, 4), (early, heads)),
    ]


def parcels_of(heads):
    group = 2 if heads % 2 == 0 else 1
    pairs = [(low, low + group) for low in range(0, heads, group)]
    return (
        [((0, 2), pair) for pair in pairs]
        + [part for pair in pairs[:-1] for part in (((2, 3), pair), ((3, 4), pair))]
        + [((2, 3), pairs[-1])]
        + [((3, 4), (head, head + 1)) for head in range(*pairs[-1])]
    )


def solution(mesh):
    nz, nd = mesh.shape["head"], mesh.shape["doc"]

    def local(queries, keys, values, log_decay, beta_logit, block_owner, block_start, gain):
        tok, channels = queries.shape
        heads = channels // WIDTH // nz
        rowtok = tok * nz
        slots = 2 * rowtok
        tiles = rowtok // TILE
        shared = nz % 2 == 0 and tiles == 2 and tok * (nz // 2) == TILE and heads >= HIGH_HOME + 2
        group = heads - LOW_HOME if shared else 2 if heads % 2 == 0 else 1
        parcels = parcels_of(heads)
        most, both = max(LOW_HOME, HIGH_HOME), LOW_HOME + HIGH_HOME
        anywhere = pl.BlockSpec(memory_space=pl.ANY)
        dma = pltpu.SemaphoreType.DMA
        return pl.pallas_call(
            functools.partial(kernel, nz, nd, parcels, shared),
            out_shape=pltpu.VMEM((slots, heads * WIDTH), BF16),
            in_specs=[anywhere] * 8,
            out_specs=pl.BlockSpec(memory_space=pltpu.VMEM),
            scratch_shapes=[
                pltpu.VMEM((4, rowtok, heads * WIDTH), BF16),
                pltpu.VMEM((4, tok, channels), BF16),
                pltpu.VMEM((nz, beta_logit.shape[1], tok), BF16),
                pltpu.VMEM(block_owner.shape, jnp.int32),
                pltpu.VMEM(block_start.shape, jnp.int32),
                pltpu.VMEM((1, heads * WIDTH), F32),
                pltpu.VMEM((rowtok, beta_logit.shape[1]), F32),
                pltpu.VMEM((beta_logit.shape[1], rowtok), F32),
                pltpu.VMEM((slots, rowtok), BF16),
                pltpu.VMEM((heads, slots, WIDTH), BF16),
                pltpu.VMEM((rowtok, WIDTH), F32),
                pltpu.VMEM((tiles, 2, TILE, TILE), F32),
                pltpu.VMEM((heads, rowtok, WIDTH), F32),
                pltpu.VMEM((heads, rowtok, WIDTH), F32),
                pltpu.VMEM((heads, rowtok, WIDTH), F32),
                pltpu.VMEM((heads, tiles, 8, WIDTH), F32),
                pltpu.VMEM((heads, rowtok, WIDTH), F32),
                pltpu.VMEM((heads, tiles, WIDTH, WIDTH), F32),
                pltpu.VMEM((heads, tiles, WIDTH, WIDTH), F32),
                pltpu.VMEM((group, rowtok, 2 * rowtok), BF16),
                pltpu.VMEM((heads, slots, 2 * rowtok), BF16),
                dma((16,)),
                dma((nz, len(parcels))),
                dma((nz, len(parcels))),
                dma((nz,)),
                dma((nz,)),
                dma((RUNS, heads)),
                dma((RUNS, heads)),
                pltpu.SemaphoreType.REGULAR,
                pltpu.SemaphoreType.REGULAR,
            ]
            + [
                pltpu.VMEM((4, TILE, most * WIDTH), BF16),
                pltpu.VMEM((1, heads * WIDTH), F32),
                pltpu.VMEM((both, TILE, WIDTH), jnp.int16),
                pltpu.VMEM((both, TILE, WIDTH), jnp.int16),
                pltpu.VMEM((both, 8, WIDTH), F32),
                pltpu.VMEM((both, 8, WIDTH), F32),
                pltpu.VMEM((most, TILE, WIDTH), BF16),
                pltpu.VMEM((most, TILE, WIDTH), BF16),
                pltpu.VMEM((most, TILE, WIDTH), BF16),
                pltpu.VMEM((both, TILE, WIDTH), F32),
                pltpu.VMEM((both, TILE, WIDTH), F32),
                dma((nz, 2)),
                dma((nz, 2)),
                dma((6,)),
                dma((6,)),
            ]
            * shared,
            compiler_params=pltpu.CompilerParams(
                collective_id=0, has_side_effects=True, vmem_limit_bytes=60 * 1024 * 1024
            ),
            name="delta",
        )(
            queries, keys, values, log_decay, beta_logit.T, block_owner, block_start,
            gain.reshape(1, -1),
        )

    return jax.shard_map(
        local,
        mesh=mesh,
        in_specs=(P(("doc", "head"), None),) * 5 + (P(), P(), P("head")),
        out_specs=P("doc", "head"),
        check_vma=False,
    )
```

```python
import functools

import jax
import jax.numpy as jnp
from jax import lax
from jax.experimental import pallas as pl
from jax.experimental.pallas import tpu as pltpu
from jax.sharding import PartitionSpec as P

WIDTH = 128
BLOCK = 16
TILE = 128
RUNS = 4
BASE = 16
AHEAD = 3
LOW_HOME, HIGH_HOME = 1, 2
AT_ONCE = {True: (), False: ()}
AFTER_ONE = {True: (1, 2, 3), False: (1, 2)}
AFTER_TWO = {True: (4,), False: (3, 4)}
AFTER = {True: ((), (), (), (), ()), False: ((), (), (), (), ())}
CLOSE_AT = {True: 1, False: 2}

MESH = pl.DeviceIdType.MESH
F32 = jnp.float32
BF16 = jnp.bfloat16
NN = (((1,), (0,)), ((), ()))
NT = (((1,), (1,)), ((), ()))
TN = (((0,), (0,)), ((), ()))


def split(x):
    high = x.astype(BF16)
    return high, (x - high.astype(F32)).astype(BF16)


def bdot(a, b, dims=NN):
    return lax.dot_general(a, b, dims, preferred_element_type=F32)


def dot3(a, b, dims=NN):
    a_high, a_low = split(a) if not isinstance(a, tuple) else a
    b_high, b_low = split(b) if not isinstance(b, tuple) else b
    ca, cb = dims[0][0][0], dims[0][1][0]
    left = jnp.concatenate([a_high, a_low], axis=ca)
    free = 1 - cb
    top = jnp.concatenate([b_high, b_low], axis=free)
    bottom = jnp.concatenate([b_high, jnp.zeros_like(b_low)], axis=free)
    both = bdot(left, jnp.concatenate([top, bottom], axis=cb), dims)
    width = both.shape[1] // 2
    return both[:, :width] + both[:, width:]


def lane_iota(shape):
    return lax.broadcasted_iota(jnp.int32, shape, 1)


def row_iota(shape):
    return lax.broadcasted_iota(jnp.int32, shape, 0)


def neumann(neg, order, eye):
    power = [dot3(n, n) for n in neg]
    total = [eye + n for n in neg]
    size = 2
    while size < order:
        if size * 2 >= order:
            total = [x + dot3(x, p) for x, p in zip(total, power)]
        else:
            both = [dot3(jnp.concatenate([x, p], axis=0), p) for x, p in zip(total, power)]
            total = [x + b[:TILE] for x, b in zip(total, both)]
            power = [b[TILE:] for b in both]
        size *= 2
    return total


def inverses(mats):
    shape = (TILE, TILE)
    row, col = row_iota(shape), lane_iota(shape)
    eye = (row == col).astype(F32)
    diag = row // BASE == col // BASE
    inner = neumann([jnp.where(diag, -a, 0.0) for a in mats], BASE, eye)
    parts = [split(x) for x in inner]
    outer = [-dot3(p, jnp.where(diag, 0.0, a)) for p, a in zip(parts, mats)]
    return [dot3(y, p) for y, p in zip(neumann(outer, TILE // BASE, eye), parts)]


def rows_of(steps, body):
    if steps <= 4:
        for step in range(steps):
            body(step)
    else:
        lax.fori_loop(0, steps, lambda step, carry: (body(step), carry)[1], 0)


def kernel(
    nz, nd, parcels, shared, q_ref, k_ref, v_ref, g_ref, b_ref, owner_in, start_in, gain_in, out_ref,
    buf, held, bbuf, owner_ref, start_ref, gain_ref, betas, brows, place, stage, segcol, masks,
    growth, keyinv, keystate, halves, weights, ends, carries, mats, placed,
    local_sem, send_sem, recv_sem, bsend_sem, brecv_sem, osend_sem, orecv_sem,
    row_sem, all_sem, *rest,
):
    me = lax.axis_index("head")
    doc = lax.axis_index("doc")
    _, rowtok, columns = buf.shape
    heads = columns // WIDTH
    tok = q_ref.shape[0]
    nblk = rowtok // BLOCK
    cap = 2 * nblk // RUNS
    capt = cap * BLOCK
    tiles = rowtok // TILE
    slots = RUNS * capt
    shape = (TILE, TILE)
    refs = (k_ref, g_ref, q_ref, v_ref)

    def greet(semaphore):
        for step in peers:
            pl.semaphore_signal(
                semaphore, inc=1, device_id={"doc": lax.rem(doc + step, nd)}, device_id_type=MESH
            )

    barrier = pltpu.get_barrier_semaphore()
    count = 0
    for step in range(1, nz):
        pl.semaphore_signal(
            barrier, inc=1, device_id={"head": lax.rem(me + step, nz)}, device_id_type=MESH
        )
        count += 1
    peers = sorted({s % nd for s in range(1, RUNS)} | {(-s) % nd for s in range(1, RUNS)})
    leader = me == 0

    @pl.when(leader)
    def _():
        greet(barrier)


    mine = pl.ds(pl.multiple_of(me * tok, tok), tok)
    own = pl.ds(pl.multiple_of(me * columns, columns), columns)
    fetch = [pltpu.make_async_copy(refs[w], held.at[w], local_sem.at[w]) for w in range(4)]
    small = [
        pltpu.make_async_copy(source, target, local_sem.at[4 + index])
        for index, (source, target) in enumerate(
            [(owner_in, owner_ref), (start_in, start_ref), (gain_in, gain_ref), (b_ref, bbuf.at[me])]
        )
    ]
    keep = [
        pltpu.make_async_copy(refs[w].at[:, own], buf.at[w, mine, :], local_sem.at[8 + w])
        for w in range(4)
    ]
    half = nz // 2
    below = me < half
    base = jnp.where(below, 0, half)
    mate = jnp.where(below, me + half, me - half)
    if shared:
        (
            fbuf, fgain, codes, coded, sizes, sized, give, got, near, reads, frees,
            fsend, frecv, xsend, xrecv,
        ) = rest
        seat = pl.ds(pl.multiple_of((me - base) * tok, tok), tok)
        theirs = pl.ds(pl.multiple_of(mate * columns, columns), fbuf.shape[2])
        keep += [
            pltpu.make_async_copy(refs[w].at[:, theirs], fbuf.at[w, seat, :], local_sem.at[12 + w])
            for w in range(4)
        ]
    for copy in fetch + small + keep:
        copy.start()
    for copy in small:
        copy.wait()
    here = row_iota((nd, nblk)) == doc
    owner = jnp.sum(jnp.where(here, owner_ref[...], 0), axis=0, keepdims=True)
    start = jnp.sum(jnp.where(here, start_ref[...], 0), axis=0, keepdims=True)
    eye_b = row_iota((nblk, nblk)) == lane_iota((nblk, nblk))
    owner_col = jnp.sum(jnp.where(eye_b, owner, 0), axis=1, keepdims=True)
    earlier = row_iota((nblk, nblk)) < lane_iota((nblk, nblk))
    rank = jnp.sum(jnp.where(earlier & (owner_col == owner), 1, 0), axis=0, keepdims=True)
    ahead = owner - doc
    ahead = jnp.where(ahead < 0, ahead + nd, ahead)
    slot = (ahead * cap + rank).astype(F32).astype(BF16)
    token_block = lane_iota((nblk, rowtok)) // BLOCK
    expand = (row_iota((nblk, rowtok)) == token_block).astype(F32).astype(BF16)
    slot_tok = bdot(slot, expand).astype(jnp.int32) * BLOCK + lane_iota((1, rowtok)) % BLOCK
    place[...] = (row_iota((slots, rowtok)) == slot_tok).astype(F32).astype(BF16)
    upto = (row_iota((nblk, rowtok)) <= token_block).astype(F32).astype(BF16)
    seg_row = bdot(start.astype(F32).astype(BF16), upto)
    seg_col = jnp.sum(
        jnp.where(
            lane_iota((rowtok, nblk)) <= row_iota((rowtok, nblk)) // BLOCK, start.astype(F32), 0.0
        ),
        axis=1,
        keepdims=True,
    )
    segcol[...] = jnp.broadcast_to(seg_col, (rowtok, WIDTH))
    for tile in range(tiles):
        lo = tile * TILE
        same = seg_col[lo : lo + TILE] == seg_row[:, lo : lo + TILE]
        masks[tile, 0] = (same & (row_iota(shape) > lane_iota(shape))).astype(F32)
        masks[tile, 1] = (same & (row_iota(shape) >= lane_iota(shape))).astype(F32)
    for tile in range(tiles - 1):
        lo = tile * TILE
        for part in range(2):
            wide = pl.ds(part * rowtok + lo + TILE, rowtok - lo - TILE)
            mats[:, lo : lo + TILE, wide] = jnp.zeros(
                (mats.shape[0], TILE, rowtok - lo - TILE), BF16
            )

    for copy in fetch:
        copy.wait()

    @pl.when(leader)
    def _():
        pl.semaphore_wait(barrier, count + len(peers))
        greet(row_sem)

    @pl.when(me != 0)
    def _():
        pl.semaphore_wait(barrier, count)

    def incoming(step, parcel):
        (first, last), (low, high) = parcels[parcel]
        partner = lax.rem(me + step, nz)
        begin = pl.multiple_of(partner * columns + low * WIDTH, WIDTH)
        return pltpu.make_async_remote_copy(
            src_ref=held.at[first:last, :, pl.ds(begin, (high - low) * WIDTH)],
            dst_ref=buf.at[first:last, mine, low * WIDTH : high * WIDTH],
            send_sem=send_sem.at[step, parcel],
            recv_sem=recv_sem.at[step, parcel],
            device_id={"head": partner},
            device_id_type=MESH,
        )

    def incoming_beta(step):
        return pltpu.make_async_remote_copy(
            src_ref=b_ref,
            dst_ref=bbuf.at[me],
            send_sem=bsend_sem.at[step],
            recv_sem=brecv_sem.at[step],
            device_id={"head": lax.rem(me + step, nz)},
            device_id_type=MESH,
        )

    def outgoing(run, head):
        rows = pl.ds(run * capt, capt)
        return pltpu.make_async_remote_copy(
            src_ref=stage.at[head, rows, :],
            dst_ref=out_ref.at[rows, pl.ds(pl.multiple_of(head * WIDTH, WIDTH), WIDTH)],
            send_sem=osend_sem.at[run, head],
            recv_sem=orecv_sem.at[run, head],
            device_id={"doc": lax.rem(doc + run, nd)},
            device_id_type=MESH,
        )

    steps = sorted(range(1, nz), key=lambda s: (-min(s, nz - s), s))
    cross = list(range(nz - 1, half - 1, -1))
    beside = list(range(1, half))
    kinds = {True: LOW_HOME, False: HIGH_HOME}

    def person(step):
        if step < half:
            return base + lax.rem(me - base + step, half)
        return half - base + lax.rem(me - base + step - half, half)

    def parcel_to(low, step, index):
        (first, last), (begin, end) = homes(heads, kinds[low])[index]
        partner = person(step)
        column = pl.multiple_of(partner * columns + begin * WIDTH, WIDTH)
        return pltpu.make_async_remote_copy(
            src_ref=held.at[first:last, :, pl.ds(column, (end - begin) * WIDTH)],
            dst_ref=buf.at[first:last, mine, begin * WIDTH : end * WIDTH],
            send_sem=send_sem.at[step, index],
            recv_sem=recv_sem.at[step, index],
            device_id={"head": partner},
            device_id_type=MESH,
        )

    def early_own(low, step):
        wide = kinds[low] * WIDTH
        partner = person(step)
        return pltpu.make_async_remote_copy(
            src_ref=held.at[:, :, pl.ds(pl.multiple_of(partner * columns, WIDTH), wide)],
            dst_ref=buf.at[:, mine, 0:wide],
            send_sem=fsend.at[step, 0],
            recv_sem=frecv.at[step, 0],
            device_id={"head": partner},
            device_id_type=MESH,
        )

    def early_other(low, step):
        wide = kinds[not low] * WIDTH
        partner = person(step)
        origin = half - base + partner - base
        return pltpu.make_async_remote_copy(
            src_ref=held.at[:, :, pl.ds(pl.multiple_of(origin * columns, WIDTH), wide)],
            dst_ref=fbuf.at[:, seat, 0:wide],
            send_sem=fsend.at[step, 1],
            recv_sem=frecv.at[step, 1],
            device_id={"head": partner},
            device_id_type=MESH,
        )

    def to_mate(source, target, index):
        return pltpu.make_async_remote_copy(
            src_ref=source,
            dst_ref=target,
            send_sem=xsend.at[index],
            recv_sem=xrecv.at[index],
            device_id={"head": mate},
            device_id_type=MESH,
        )

    def gain_over():
        return to_mate(gain_ref, fgain, 0)

    def states_over(part):
        some = pl.ds(0, LOW_HOME) if part == 0 else pl.ds(LOW_HOME, HIGH_HOME)
        return [
            to_mate(sizes.at[some], sized.at[some], 4 + part),
            to_mate(codes.at[some], coded.at[some], 1 + part),
        ]

    def half_over(low):
        count = kinds[not low]
        return to_mate(give.at[0:count], got.at[0:count], 3)

    def send_parcels(low, index):
        for step in cross:
            parcel_to(not low, step, index).start()
        for step in beside:
            parcel_to(low, step, index).start()

    for step in steps:
        incoming_beta(step).start()
    if shared:

        def begin_sends(low):
            for step in beside:
                (early_own if low else early_other)(low, step).start()
            for step in cross:
                parcel_to(not low, step, 0).start()
            for step in beside:
                (early_other if low else early_own)(low, step).start()
            for step in beside:
                parcel_to(low, step, 0).start()
            for index in AT_ONCE[low]:
                send_parcels(low, index)

        @pl.when(below)
        def _():
            begin_sends(True)

        @pl.when(jnp.logical_not(below))
        def _():
            begin_sends(False)

    else:
        for parcel in range(min(AHEAD, len(parcels))):
            for step in steps:
                incoming(step, parcel).start()

    if shared:
        gain_over().start()
    for step in range(1, nz):
        incoming_beta(step).wait_recv()

    eye_tok = (row_iota((tok, tok)) == lane_iota((tok, tok))).astype(F32).astype(BF16)
    flat = jnp.zeros((bbuf.shape[1], rowtok), F32)
    for step in range(nz):
        turned = bdot(eye_tok, bbuf[step], NT)
        betas[step * tok : (step + 1) * tok, :] = jax.nn.sigmoid(turned)
        shift = row_iota((tok, rowtok)) + step * tok == lane_iota((tok, rowtok))
        flat = flat + bdot(bbuf[step], shift.astype(F32).astype(BF16))
    brows[...] = jax.nn.sigmoid(flat)

    for copy in keep:
        copy.wait()

    @pl.when(leader)
    def _():
        pl.semaphore_wait(row_sem, len(peers))
        for step in range(1, nz):
            pl.semaphore_signal(
                all_sem, inc=1, device_id={"head": lax.rem(me + step, nz)}, device_id_type=MESH
            )

    @pl.when(me != 0)
    def _():
        pl.semaphore_wait(all_sem, 1)

    def arrive(parcel):
        for step in range(1, nz):
            incoming(step, parcel).wait_recv()

    def beta_of(head):
        values = betas[...]
        mine_here = lane_iota(values.shape) == me * heads + head
        return jnp.sum(jnp.where(mine_here, values, 0.0), axis=1, keepdims=True)

    def before(tile):
        return segcol[tile * TILE - 1 : tile * TILE, :]

    def final(tile):
        return segcol[(tile + 1) * TILE - 1 : (tile + 1) * TILE, :]

    def lanes(head):
        return pl.ds(head * WIDTH, WIDTH)

    def keys_part(members):
        lower = (row_iota(shape) >= lane_iota(shape)).astype(F32).astype(BF16)
        where, amats, tails = [], [], []
        for head in members:
            beta = beta_of(head)
            for tile in range(tiles):
                rows = pl.ds(tile * TILE, TILE)
                seg = segcol[rows, :]
                key = buf[0, rows, lanes(head)].astype(F32)
                key = key * lax.rsqrt(jnp.sum(key * key, axis=-1, keepdims=True) + 1e-06)
                cumul = bdot(lower, buf[1, rows, lanes(head)])
                half = 0.5 * cumul[TILE - 1 :, :]
                grow = jnp.exp(cumul - half)
                middle = jnp.exp(half)
                kg, ki = key * grow, key * jnp.exp(half - cumul)
                amat = dot3(kg, ki, NT)
                amat = jnp.where(masks[tile, 0] > 0.0, amat, 0.0)
                amats.append(amat * beta[tile * TILE : (tile + 1) * TILE])
                where.append((head, tile, rows))
                growth[head, rows, :] = grow
                keyinv[head, rows, :] = ki
                halves[head, tile] = jnp.broadcast_to(middle, (8, WIDTH))
                if tile > 0:
                    keystate[head, rows, :] = kg * ((seg == before(tile)).astype(F32) * middle)
                tails.append(ki * ((seg == final(tile)).astype(F32) * middle))
        solved = []
        for (head, tile, rows), inv in zip(where, inverses(amats)):
            row = brows[pl.ds(me * heads + head, 1), :]
            scaled = inv * row[:, tile * TILE : (tile + 1) * TILE]
            weights[head, rows, :] = scaled
            solved.append(scaled)
        made = [
            dot3(t, w, TN) if tile < tiles - 1 else None
            for (head, tile, rows), t, w in zip(where, tails, solved)
        ]
        for (head, tile, rows), end in zip(where, made):
            if tile < tiles - 1:
                ends[head, tile] = end
                if tile > 0:
                    middle = halves[head, tile, 0:1, :]
                    scale = middle * middle * (final(tile) == before(tile)).astype(F32)
                    eye = row_iota(shape) == lane_iota(shape)
                    carries[head, tile] = jnp.where(eye, scale, 0.0) - dot3(
                        end, keystate[head, rows, :]
                    )

    def store(index, tile, source, block):
        high, low = split(block)
        rows = pl.ds(tile * TILE, TILE)
        mats[index, rows, pl.ds(source * TILE, TILE)] = high
        mats[index, rows, pl.ds(rowtok + source * TILE, TILE)] = low

    def queries_part(members):
        where, grown, scores = [], [], []
        for index, head in enumerate(members):
            for tile in range(tiles):
                rows = pl.ds(tile * TILE, TILE)
                query = buf[2, rows, lanes(head)].astype(F32)
                query = (
                    query
                    * lax.rsqrt(jnp.sum(query * query, axis=-1, keepdims=True) + 1e-06)
                    * WIDTH ** (-0.5)
                )
                qg = query * growth[head, rows, :]
                score = dot3(qg, keyinv[head, rows, :], NT)
                scores.append(jnp.where(masks[tile, 1] > 0.0, score, 0.0))
                grown.append(qg)
                where.append((index, head, tile, rows))
        inner = [
            dot3(score, weights[head, rows, :])
            for (index, head, tile, rows), score in zip(where, scores)
        ]
        reads = []
        for (index, head, tile, rows), block, qg in zip(where, inner, grown):
            store(index, tile, tile, block)
            if tile > 0:
                first = (segcol[rows, :] == before(tile)).astype(F32) * halves[head, tile, 0:1, :]
                reads.append(qg * first - dot3(block, keystate[head, rows, :]))
            else:
                reads.append(None)
        for index, head in enumerate(members):
            for source in range(tiles - 1):
                state = ends[head, source]
                for tile in range(source + 1, tiles):
                    parts = split(state)
                    store(index, tile, source, dot3(reads[index * tiles + tile], parts))
                    if tile < tiles - 1:
                        state = dot3(carries[head, tile], parts)
        for index, head in enumerate(members):

            def move(step):
                rows = pl.ds(pl.multiple_of(step * TILE, TILE), TILE)
                placed[head, rows, :] = bdot(place[rows, :], mats[index]).astype(BF16)

            rows_of(slots // TILE, move)

    def values_part(head):
        value = buf[3, :, lanes(head)]
        value = jnp.concatenate([value, value], axis=0)
        gain = gain_ref[:, lanes(head)]
        for run in list(range(2, RUNS)) + [1, 0]:
            rows = pl.ds(run * capt, capt)
            result = bdot(placed[head, rows, :], value)
            norm = lax.rsqrt(jnp.mean(result * result, axis=-1, keepdims=True) + 1e-05)
            result = (result * norm * gain).astype(BF16)
            if run == 0:
                out_ref[rows, lanes(head)] = result
            else:
                stage[head, rows, :] = result
                outgoing(run, head).start()

    def of_value(matrix, value):
        high, low = split(matrix)
        return bdot(
            jnp.concatenate([high, low], axis=1), jnp.concatenate([value, value], axis=0)
        )

    def normed(result, gain):
        norm = lax.rsqrt(jnp.mean(result * result, axis=-1, keepdims=True) + 1e-05)
        return (result * norm * gain).astype(BF16)

    def tile_part(tile, items):
        rows = slice(tile * TILE, (tile + 1) * TILE)
        lower = (row_iota(shape) >= lane_iota(shape)).astype(F32).astype(BF16)
        seg = segcol[rows, :]
        kept, amats = [], []
        for load, place_of in items:
            values = betas[rows, :]
            beta = jnp.sum(
                jnp.where(lane_iota(values.shape) == place_of, values, 0.0), axis=1, keepdims=True
            )
            key = load(0).astype(F32)
            key = key * lax.rsqrt(jnp.sum(key * key, axis=-1, keepdims=True) + 1e-06)
            cumul = bdot(lower, load(1))
            mid = 0.5 * cumul[TILE - 1 :, :]
            grow = jnp.exp(cumul - mid)
            middle = jnp.exp(mid)
            kg, ki = key * grow, key * jnp.exp(mid - cumul)
            amat = jnp.where(masks[tile, 0] > 0.0, dot3(kg, ki, NT), 0.0)
            amats.append(amat * beta)
            query = load(2).astype(F32)
            query = (
                query
                * lax.rsqrt(jnp.sum(query * query, axis=-1, keepdims=True) + 1e-06)
                * WIDTH ** (-0.5)
            )
            qg = query * grow
            score = jnp.where(masks[tile, 1] > 0.0, dot3(qg, ki, NT), 0.0)
            kept.append((kg, ki, middle, qg, score))
        solved = [
            inv * brows[pl.ds(place_of, 1), :][:, rows]
            for (load, place_of), inv in zip(items, inverses(amats))
        ]
        inner = [dot3(score, w) for (kg, ki, middle, qg, score), w in zip(kept, solved)]
        if tile == 0:
            outer = [
                dot3(ki * ((seg == final(0)).astype(F32) * middle), w, TN)
                for (kg, ki, middle, qg, score), w in zip(kept, solved)
            ]
        else:
            outer = []
            for (kg, ki, middle, qg, score), block in zip(kept, inner):
                first = (seg == before(tile)).astype(F32) * middle
                outer.append(qg * first - dot3(block, kg * first))
        return inner, outer

    def put(head, both):
        full = bdot(place[...], both).astype(BF16)
        for run in list(range(2, RUNS)) + [1, 0]:
            rows = pl.ds(run * capt, capt)
            piece = full[run * capt : (run + 1) * capt]
            if run == 0:
                out_ref[rows, lanes(head)] = piece
            else:
                stage[head, rows, :] = piece
                outgoing(run, head).start()

    def role(low):
        home, other = kinds[low], kinds[not low]
        tile = 0 if low else 1
        area = slice(tile * TILE, (tile + 1) * TILE)

        def from_own(head):
            return (lambda w: buf[w, area, lanes(head)]), me * heads + head

        def from_other(head):
            return (lambda w: fbuf[w, :, lanes(head)]), mate * heads + head

        def settle(index):
            for step in cross + beside:
                parcel_to(low, step, index).wait_recv()

        def meet(part):
            for copy in states_over(part):
                copy.wait_recv()
            for slot in range(other) if part == 0 else range(other, home + other):
                result = (
                    dot3(reads[slot], coded[slot].astype(jnp.int32).astype(F32))
                    * sized[slot, 0:1, :]
                    + frees[slot]
                )
                if part == 0:
                    give[slot] = normed(result, fgain[:, lanes(slot)])
                else:
                    near[slot - other] = normed(result, gain_ref[:, lanes(slot - other)])
            if part == 0:
                half_over(low).start()

        def close():
            half_over(not low).wait_recv()
            for head in range(home):
                ordered = [near[head], got[head]] if low else [got[head], near[head]]
                put(head, jnp.concatenate(ordered, axis=0))

        def early(own, step):
            return early_own(low, step) if own else early_other(low, step)

        def phase(part):
            own = low == (part == 0)
            if own:
                items = [from_own(head) for head in range(home)]
            else:
                items = [from_other(head) for head in range(other)]
            shift = 0 if part == 0 else LOW_HOME
            for step in beside:
                early(own, step).wait_recv()
            inner, outer = tile_part(tile, items)
            values = [load(3) for load, place_of in items]
            if low:
                for slot, (block, value) in enumerate(zip(outer, values)):
                    state = of_value(block, value)
                    most = jnp.maximum(jnp.max(jnp.abs(state), axis=0, keepdims=True), 1e-30)
                    code = jnp.round(state * (32767.0 / most)).astype(jnp.int32)
                    codes[shift + slot] = code.astype(jnp.int16)
                    sizes[shift + slot] = jnp.broadcast_to(most * (1.0 / 32767.0), (8, WIDTH))
                for copy in states_over(part):
                    copy.start()
            for slot, (block, value) in enumerate(zip(inner, values)):
                result = of_value(block, value)
                if not low:
                    reads[shift + slot] = outer[slot]
                    frees[shift + slot] = result
                elif own:
                    near[slot] = normed(result, gain_ref[:, lanes(slot)])
                else:
                    give[slot] = normed(result, fgain[:, lanes(slot)])
            if low and not own:
                half_over(low).start()

        phase(0)
        for index in AFTER_ONE[low]:
            send_parcels(low, index)
        gain_over().wait_recv()
        phase(1)
        if not low:
            meet(0)
        for index in AFTER_TWO[low]:
            send_parcels(low, index)

        plan = homes(heads, home)
        for index, ((first, last), (begin, end)) in enumerate(plan):
            settle(index)
            for later in AFTER[low][index]:
                send_parcels(low, later)
            if first == 0:
                keys_part(list(range(begin, end)))
            elif first == 2:
                queries_part(list(range(begin, end)))
            else:
                for head in range(begin, end):
                    values_part(head)
            if index == CLOSE_AT[low]:
                if not low:
                    meet(1)
                close()
        for index in range(len(plan)):
            for step in beside:
                parcel_to(low, step, index).wait_send()
            for step in cross:
                parcel_to(not low, step, index).wait_send()
        for step in beside:
            early_own(low, step).wait_send()
            early_other(low, step).wait_send()
        if low:
            for copy in states_over(0) + states_over(1):
                copy.wait_send()
        gain_over().wait_send()
        half_over(low).wait_send()

    if shared:

        @pl.when(below)
        def _():
            role(True)

        @pl.when(jnp.logical_not(below))
        def _():
            role(False)

    else:
        group = mats.shape[0]
        for parcel, ((first, last), (low, high)) in enumerate(parcels):
            arrive(parcel)
            if parcel + AHEAD < len(parcels):
                for step in steps:
                    incoming(step, parcel + AHEAD).start()
            for begin in range(low, high, group):
                members = list(range(begin, min(begin + group, high)))
                if first == 0:
                    keys_part(members)
                if first <= 2 < last:
                    queries_part(members)
            if last == 4:
                for head in range(low, high):
                    values_part(head)

    for step in range(1, nz):
        incoming_beta(step).wait_send()
        for parcel in range(0 if shared else len(parcels)):
            incoming(step, parcel).wait_send()
    for head in range(heads):
        for run in range(1, RUNS):
            outgoing(run, head).wait()


def homes(heads, begin):
    early = heads - 1
    return [
        ((0, 2), (begin, heads)),
        ((2, 3), (begin, early)),
        ((3, 4), (begin, early)),
        ((2, 3), (early, heads)),
        ((3, 4), (early, heads)),
    ]


def parcels_of(heads):
    group = 2 if heads % 2 == 0 else 1
    pairs = [(low, low + group) for low in range(0, heads, group)]
    return (
        [((0, 2), pair) for pair in pairs]
        + [part for pair in pairs[:-1] for part in (((2, 3), pair), ((3, 4), pair))]
        + [((2, 3), pairs[-1])]
        + [((3, 4), (head, head + 1)) for head in range(*pairs[-1])]
    )


def solution(mesh):
    nz, nd = mesh.shape["head"], mesh.shape["doc"]

    def local(queries, keys, values, log_decay, beta_logit, block_owner, block_start, gain):
        tok, channels = queries.shape
        heads = channels // WIDTH // nz
        rowtok = tok * nz
        slots = 2 * rowtok
        tiles = rowtok // TILE
        shared = nz % 2 == 0 and tiles == 2 and tok * (nz // 2) == TILE and heads >= HIGH_HOME + 2
        group = heads - LOW_HOME if shared else 2 if heads % 2 == 0 else 1
        parcels = parcels_of(heads)
        most, both = max(LOW_HOME, HIGH_HOME), LOW_HOME + HIGH_HOME
        anywhere = pl.BlockSpec(memory_space=pl.ANY)
        dma = pltpu.SemaphoreType.DMA
        return pl.pallas_call(
            functools.partial(kernel, nz, nd, parcels, shared),
            out_shape=pltpu.VMEM((slots, heads * WIDTH), BF16),
            in_specs=[anywhere] * 8,
            out_specs=pl.BlockSpec(memory_space=pltpu.VMEM),
            scratch_shapes=[
                pltpu.VMEM((4, rowtok, heads * WIDTH), BF16),
                pltpu.VMEM((4, tok, channels), BF16),
                pltpu.VMEM((nz, beta_logit.shape[1], tok), BF16),
                pltpu.VMEM(block_owner.shape, jnp.int32),
                pltpu.VMEM(block_start.shape, jnp.int32),
                pltpu.VMEM((1, heads * WIDTH), F32),
                pltpu.VMEM((rowtok, beta_logit.shape[1]), F32),
                pltpu.VMEM((beta_logit.shape[1], rowtok), F32),
                pltpu.VMEM((slots, rowtok), BF16),
                pltpu.VMEM((heads, slots, WIDTH), BF16),
                pltpu.VMEM((rowtok, WIDTH), F32),
                pltpu.VMEM((tiles, 2, TILE, TILE), F32),
                pltpu.VMEM((heads, rowtok, WIDTH), F32),
                pltpu.VMEM((heads, rowtok, WIDTH), F32),
                pltpu.VMEM((heads, rowtok, WIDTH), F32),
                pltpu.VMEM((heads, tiles, 8, WIDTH), F32),
                pltpu.VMEM((heads, rowtok, WIDTH), F32),
                pltpu.VMEM((heads, tiles, WIDTH, WIDTH), F32),
                pltpu.VMEM((heads, tiles, WIDTH, WIDTH), F32),
                pltpu.VMEM((group, rowtok, 2 * rowtok), BF16),
                pltpu.VMEM((heads, slots, 2 * rowtok), BF16),
                dma((16,)),
                dma((nz, len(parcels))),
                dma((nz, len(parcels))),
                dma((nz,)),
                dma((nz,)),
                dma((RUNS, heads)),
                dma((RUNS, heads)),
                pltpu.SemaphoreType.REGULAR,
                pltpu.SemaphoreType.REGULAR,
            ]
            + [
                pltpu.VMEM((4, TILE, most * WIDTH), BF16),
                pltpu.VMEM((1, heads * WIDTH), F32),
                pltpu.VMEM((both, TILE, WIDTH), jnp.int16),
                pltpu.VMEM((both, TILE, WIDTH), jnp.int16),
                pltpu.VMEM((both, 8, WIDTH), F32),
                pltpu.VMEM((both, 8, WIDTH), F32),
                pltpu.VMEM((most, TILE, WIDTH), BF16),
                pltpu.VMEM((most, TILE, WIDTH), BF16),
                pltpu.VMEM((most, TILE, WIDTH), BF16),
                pltpu.VMEM((both, TILE, WIDTH), F32),
                pltpu.VMEM((both, TILE, WIDTH), F32),
                dma((nz, 2)),
                dma((nz, 2)),
                dma((6,)),
                dma((6,)),
            ]
            * shared,
            compiler_params=pltpu.CompilerParams(
                collective_id=0, has_side_effects=True, vmem_limit_bytes=60 * 1024 * 1024
            ),
            name="delta",
        )(
            queries, keys, values, log_decay, beta_logit.T, block_owner, block_start,
            gain.reshape(1, -1),
        )

    return jax.shard_map(
        local,
        mesh=mesh,
        in_specs=(P(("doc", "head"), None),) * 5 + (P(), P(), P("head")),
        out_specs=P("doc", "head"),
        check_vma=False,
    )
```

```python
import functools

import jax
import jax.numpy as jnp
from jax import lax
from jax.experimental import pallas as pl
from jax.experimental.pallas import tpu as pltpu
from jax.sharding import PartitionSpec as P

WIDTH = 128
BLOCK = 16
TILE = 128
RUNS = 4
BASE = 16
AHEAD = 3
LOW_HOME, HIGH_HOME = 1, 2
AT_ONCE = {True: (), False: ()}
AFTER_ONE = {True: (1, 2, 3), False: (1, 2)}
AFTER_TWO = {True: (4,), False: (3, 4)}
AFTER = {True: ((), (), (), (), ()), False: ((), (), (), (), ())}
CLOSE_AT = {True: 1, False: 2}

MESH = pl.DeviceIdType.MESH
F32 = jnp.float32
BF16 = jnp.bfloat16
NN = (((1,), (0,)), ((), ()))
NT = (((1,), (1,)), ((), ()))
TN = (((0,), (0,)), ((), ()))


def split(x):
    high = x.astype(BF16)
    return high, (x - high.astype(F32)).astype(BF16)


def bdot(a, b, dims=NN):
    return lax.dot_general(a, b, dims, preferred_element_type=F32)


def dot3(a, b, dims=NN):
    a_high, a_low = split(a) if not isinstance(a, tuple) else a
    b_high, b_low = split(b) if not isinstance(b, tuple) else b
    ca, cb = dims[0][0][0], dims[0][1][0]
    left = jnp.concatenate([a_high, a_low], axis=ca)
    free = 1 - cb
    top = jnp.concatenate([b_high, b_low], axis=free)
    bottom = jnp.concatenate([b_high, jnp.zeros_like(b_low)], axis=free)
    both = bdot(left, jnp.concatenate([top, bottom], axis=cb), dims)
    width = both.shape[1] // 2
    return both[:, :width] + both[:, width:]


def lane_iota(shape):
    return lax.broadcasted_iota(jnp.int32, shape, 1)


def row_iota(shape):
    return lax.broadcasted_iota(jnp.int32, shape, 0)


def neumann(neg, order, eye):
    power = [dot3(n, n) for n in neg]
    total = [eye + n for n in neg]
    size = 2
    while size < order:
        if size * 2 >= order:
            total = [x + dot3(x, p) for x, p in zip(total, power)]
        else:
            both = [dot3(jnp.concatenate([x, p], axis=0), p) for x, p in zip(total, power)]
            total = [x + b[:TILE] for x, b in zip(total, both)]
            power = [b[TILE:] for b in both]
        size *= 2
    return total


def inverses(mats):
    shape = (TILE, TILE)
    row, col = row_iota(shape), lane_iota(shape)
    eye = (row == col).astype(F32)
    diag = row // BASE == col // BASE
    inner = neumann([jnp.where(diag, -a, 0.0) for a in mats], BASE, eye)
    parts = [split(x) for x in inner]
    outer = [-dot3(p, jnp.where(diag, 0.0, a)) for p, a in zip(parts, mats)]
    return [dot3(y, p) for y, p in zip(neumann(outer, TILE // BASE, eye), parts)]


def rows_of(steps, body):
    if steps <= 4:
        for step in range(steps):
            body(step)
    else:
        lax.fori_loop(0, steps, lambda step, carry: (body(step), carry)[1], 0)


def kernel(
    nz, nd, parcels, shared, q_ref, k_ref, v_ref, g_ref, b_ref, owner_in, start_in, gain_in, out_ref,
    buf, held, bbuf, owner_ref, start_ref, gain_ref, betas, brows, place, stage, segcol, masks,
    growth, keyinv, keystate, halves, weights, ends, carries, mats, placed,
    local_sem, send_sem, recv_sem, bsend_sem, brecv_sem, osend_sem, orecv_sem,
    row_sem, all_sem, *rest,
):
    me = lax.axis_index("head")
    doc = lax.axis_index("doc")
    _, rowtok, columns = buf.shape
    heads = columns // WIDTH
    tok = q_ref.shape[0]
    nblk = rowtok // BLOCK
    cap = 2 * nblk // RUNS
    capt = cap * BLOCK
    tiles = rowtok // TILE
    slots = RUNS * capt
    shape = (TILE, TILE)
    refs = (k_ref, g_ref, q_ref, v_ref)

    def greet(semaphore):
        for step in peers:
            pl.semaphore_signal(
                semaphore, inc=1, device_id={"doc": lax.rem(doc + step, nd)}, device_id_type=MESH
            )

    barrier = pltpu.get_barrier_semaphore()
    count = 0
    for step in range(1, nz):
        pl.semaphore_signal(
            barrier, inc=1, device_id={"head": lax.rem(me + step, nz)}, device_id_type=MESH
        )
        count += 1
    peers = sorted({s % nd for s in range(1, RUNS)} | {(-s) % nd for s in range(1, RUNS)})
    leader = me == 0

    @pl.when(leader)
    def _():
        greet(barrier)


    mine = pl.ds(pl.multiple_of(me * tok, tok), tok)
    own = pl.ds(pl.multiple_of(me * columns, columns), columns)
    fetch = [pltpu.make_async_copy(refs[w], held.at[w], local_sem.at[w]) for w in range(4)]
    small = [
        pltpu.make_async_copy(source, target, local_sem.at[4 + index])
        for index, (source, target) in enumerate(
            [(owner_in, owner_ref), (start_in, start_ref), (gain_in, gain_ref), (b_ref, bbuf.at[me])]
        )
    ]
    keep = [
        pltpu.make_async_copy(refs[w].at[:, own], buf.at[w, mine, :], local_sem.at[8 + w])
        for w in range(4)
    ]
    half = nz // 2
    below = me < half
    base = jnp.where(below, 0, half)
    mate = jnp.where(below, me + half, me - half)
    if shared:
        (
            fbuf, fgain, codes, coded, sizes, sized, give, got, near, reads, frees,
            fsend, frecv, xsend, xrecv,
        ) = rest
        seat = pl.ds(pl.multiple_of((me - base) * tok, tok), tok)
        theirs = pl.ds(pl.multiple_of(mate * columns, columns), fbuf.shape[2])
        keep += [
            pltpu.make_async_copy(refs[w].at[:, theirs], fbuf.at[w, seat, :], local_sem.at[12 + w])
            for w in range(4)
        ]
    for copy in fetch + small + keep:
        copy.start()
    for copy in fetch:
        copy.wait()

    @pl.when(leader)
    def _():
        pl.semaphore_wait(barrier, count + len(peers))
        greet(row_sem)

    @pl.when(me != 0)
    def _():
        pl.semaphore_wait(barrier, count)

    def incoming(step, parcel):
        (first, last), (low, high) = parcels[parcel]
        partner = lax.rem(me + step, nz)
        begin = pl.multiple_of(partner * columns + low * WIDTH, WIDTH)
        return pltpu.make_async_remote_copy(
            src_ref=held.at[first:last, :, pl.ds(begin, (high - low) * WIDTH)],
            dst_ref=buf.at[first:last, mine, low * WIDTH : high * WIDTH],
            send_sem=send_sem.at[step, parcel],
            recv_sem=recv_sem.at[step, parcel],
            device_id={"head": partner},
            device_id_type=MESH,
        )

    def incoming_beta(step):
        return pltpu.make_async_remote_copy(
            src_ref=b_ref,
            dst_ref=bbuf.at[me],
            send_sem=bsend_sem.at[step],
            recv_sem=brecv_sem.at[step],
            device_id={"head": lax.rem(me + step, nz)},
            device_id_type=MESH,
        )

    def outgoing(run, head):
        rows = pl.ds(run * capt, capt)
        return pltpu.make_async_remote_copy(
            src_ref=stage.at[head, rows, :],
            dst_ref=out_ref.at[rows, pl.ds(pl.multiple_of(head * WIDTH, WIDTH), WIDTH)],
            send_sem=osend_sem.at[run, head],
            recv_sem=orecv_sem.at[run, head],
            device_id={"doc": lax.rem(doc + run, nd)},
            device_id_type=MESH,
        )

    steps = sorted(range(1, nz), key=lambda s: (-min(s, nz - s), s))
    cross = list(range(nz - 1, half - 1, -1))
    beside = list(range(1, half))
    kinds = {True: LOW_HOME, False: HIGH_HOME}

    def person(step):
        if step < half:
            return base + lax.rem(me - base + step, half)
        return half - base + lax.rem(me - base + step - half, half)

    def parcel_to(low, step, index):
        (first, last), (begin, end) = homes(heads, kinds[low])[index]
        partner = person(step)
        column = pl.multiple_of(partner * columns + begin * WIDTH, WIDTH)
        return pltpu.make_async_remote_copy(
            src_ref=held.at[first:last, :, pl.ds(column, (end - begin) * WIDTH)],
            dst_ref=buf.at[first:last, mine, begin * WIDTH : end * WIDTH],
            send_sem=send_sem.at[step, index],
            recv_sem=recv_sem.at[step, index],
            device_id={"head": partner},
            device_id_type=MESH,
        )

    def early_own(low, step):
        wide = kinds[low] * WIDTH
        partner = person(step)
        return pltpu.make_async_remote_copy(
            src_ref=held.at[:, :, pl.ds(pl.multiple_of(partner * columns, WIDTH), wide)],
            dst_ref=buf.at[:, mine, 0:wide],
            send_sem=fsend.at[step, 0],
            recv_sem=frecv.at[step, 0],
            device_id={"head": partner},
            device_id_type=MESH,
        )

    def early_other(low, step):
        wide = kinds[not low] * WIDTH
        partner = person(step)
        origin = half - base + partner - base
        return pltpu.make_async_remote_copy(
            src_ref=held.at[:, :, pl.ds(pl.multiple_of(origin * columns, WIDTH), wide)],
            dst_ref=fbuf.at[:, seat, 0:wide],
            send_sem=fsend.at[step, 1],
            recv_sem=frecv.at[step, 1],
            device_id={"head": partner},
            device_id_type=MESH,
        )

    def to_mate(source, target, index):
        return pltpu.make_async_remote_copy(
            src_ref=source,
            dst_ref=target,
            send_sem=xsend.at[index],
            recv_sem=xrecv.at[index],
            device_id={"head": mate},
            device_id_type=MESH,
        )

    def gain_over():
        return to_mate(gain_ref, fgain, 0)

    def states_over(part):
        some = pl.ds(0, LOW_HOME) if part == 0 else pl.ds(LOW_HOME, HIGH_HOME)
        return [
            to_mate(sizes.at[some], sized.at[some], 4 + part),
            to_mate(codes.at[some], coded.at[some], 1 + part),
        ]

    def half_over(low):
        count = kinds[not low]
        return to_mate(give.at[0:count], got.at[0:count], 3)

    def send_parcels(low, index):
        for step in cross:
            parcel_to(not low, step, index).start()
        for step in beside:
            parcel_to(low, step, index).start()

    for step in steps:
        incoming_beta(step).start()
    if shared:

        def begin_sends(low):
            for step in beside:
                (early_own if low else early_other)(low, step).start()
            for step in cross:
                parcel_to(not low, step, 0).start()
            for step in beside:
                (early_other if low else early_own)(low, step).start()
            for step in beside:
                parcel_to(low, step, 0).start()
            for index in AT_ONCE[low]:
                send_parcels(low, index)

        @pl.when(below)
        def _():
            begin_sends(True)

        @pl.when(jnp.logical_not(below))
        def _():
            begin_sends(False)

    else:
        for parcel in range(min(AHEAD, len(parcels))):
            for step in steps:
                incoming(step, parcel).start()

    for copy in small:
        copy.wait()
    if shared:
        gain_over().start()
    here = row_iota((nd, nblk)) == doc
    owner = jnp.sum(jnp.where(here, owner_ref[...], 0), axis=0, keepdims=True)
    start = jnp.sum(jnp.where(here, start_ref[...], 0), axis=0, keepdims=True)
    eye_b = row_iota((nblk, nblk)) == lane_iota((nblk, nblk))
    owner_col = jnp.sum(jnp.where(eye_b, owner, 0), axis=1, keepdims=True)
    earlier = row_iota((nblk, nblk)) < lane_iota((nblk, nblk))
    rank = jnp.sum(jnp.where(earlier & (owner_col == owner), 1, 0), axis=0, keepdims=True)
    ahead = owner - doc
    ahead = jnp.where(ahead < 0, ahead + nd, ahead)
    slot = (ahead * cap + rank).astype(F32).astype(BF16)
    token_block = lane_iota((nblk, rowtok)) // BLOCK
    expand = (row_iota((nblk, rowtok)) == token_block).astype(F32).astype(BF16)
    slot_tok = bdot(slot, expand).astype(jnp.int32) * BLOCK + lane_iota((1, rowtok)) % BLOCK
    place[...] = (row_iota((slots, rowtok)) == slot_tok).astype(F32).astype(BF16)
    upto = (row_iota((nblk, rowtok)) <= token_block).astype(F32).astype(BF16)
    seg_row = bdot(start.astype(F32).astype(BF16), upto)
    seg_col = jnp.sum(
        jnp.where(
            lane_iota((rowtok, nblk)) <= row_iota((rowtok, nblk)) // BLOCK, start.astype(F32), 0.0
        ),
        axis=1,
        keepdims=True,
    )
    segcol[...] = jnp.broadcast_to(seg_col, (rowtok, WIDTH))
    for tile in range(tiles):
        lo = tile * TILE
        same = seg_col[lo : lo + TILE] == seg_row[:, lo : lo + TILE]
        masks[tile, 0] = (same & (row_iota(shape) > lane_iota(shape))).astype(F32)
        masks[tile, 1] = (same & (row_iota(shape) >= lane_iota(shape))).astype(F32)
    for tile in range(tiles - 1):
        lo = tile * TILE
        for part in range(2):
            wide = pl.ds(part * rowtok + lo + TILE, rowtok - lo - TILE)
            mats[:, lo : lo + TILE, wide] = jnp.zeros(
                (mats.shape[0], TILE, rowtok - lo - TILE), BF16
            )

    for step in range(1, nz):
        incoming_beta(step).wait_recv()

    eye_tok = (row_iota((tok, tok)) == lane_iota((tok, tok))).astype(F32).astype(BF16)
    flat = jnp.zeros((bbuf.shape[1], rowtok), F32)
    for step in range(nz):
        turned = bdot(eye_tok, bbuf[step], NT)
        betas[step * tok : (step + 1) * tok, :] = jax.nn.sigmoid(turned)
        shift = row_iota((tok, rowtok)) + step * tok == lane_iota((tok, rowtok))
        flat = flat + bdot(bbuf[step], shift.astype(F32).astype(BF16))
    brows[...] = jax.nn.sigmoid(flat)

    for copy in keep:
        copy.wait()

    @pl.when(leader)
    def _():
        pl.semaphore_wait(row_sem, len(peers))
        for step in range(1, nz):
            pl.semaphore_signal(
                all_sem, inc=1, device_id={"head": lax.rem(me + step, nz)}, device_id_type=MESH
            )

    @pl.when(me != 0)
    def _():
        pl.semaphore_wait(all_sem, 1)

    def arrive(parcel):
        for step in range(1, nz):
            incoming(step, parcel).wait_recv()

    def beta_of(head):
        values = betas[...]
        mine_here = lane_iota(values.shape) == me * heads + head
        return jnp.sum(jnp.where(mine_here, values, 0.0), axis=1, keepdims=True)

    def before(tile):
        return segcol[tile * TILE - 1 : tile * TILE, :]

    def final(tile):
        return segcol[(tile + 1) * TILE - 1 : (tile + 1) * TILE, :]

    def lanes(head):
        return pl.ds(head * WIDTH, WIDTH)

    def keys_part(members):
        lower = (row_iota(shape) >= lane_iota(shape)).astype(F32).astype(BF16)
        where, amats, tails = [], [], []
        for head in members:
            beta = beta_of(head)
            for tile in range(tiles):
                rows = pl.ds(tile * TILE, TILE)
                seg = segcol[rows, :]
                key = buf[0, rows, lanes(head)].astype(F32)
                key = key * lax.rsqrt(jnp.sum(key * key, axis=-1, keepdims=True) + 1e-06)
                cumul = bdot(lower, buf[1, rows, lanes(head)])
                half = 0.5 * cumul[TILE - 1 :, :]
                grow = jnp.exp(cumul - half)
                middle = jnp.exp(half)
                kg, ki = key * grow, key * jnp.exp(half - cumul)
                amat = dot3(kg, ki, NT)
                amat = jnp.where(masks[tile, 0] > 0.0, amat, 0.0)
                amats.append(amat * beta[tile * TILE : (tile + 1) * TILE])
                where.append((head, tile, rows))
                growth[head, rows, :] = grow
                keyinv[head, rows, :] = ki
                halves[head, tile] = jnp.broadcast_to(middle, (8, WIDTH))
                if tile > 0:
                    keystate[head, rows, :] = kg * ((seg == before(tile)).astype(F32) * middle)
                tails.append(ki * ((seg == final(tile)).astype(F32) * middle))
        solved = []
        for (head, tile, rows), inv in zip(where, inverses(amats)):
            row = brows[pl.ds(me * heads + head, 1), :]
            scaled = inv * row[:, tile * TILE : (tile + 1) * TILE]
            weights[head, rows, :] = scaled
            solved.append(scaled)
        made = [
            dot3(t, w, TN) if tile < tiles - 1 else None
            for (head, tile, rows), t, w in zip(where, tails, solved)
        ]
        for (head, tile, rows), end in zip(where, made):
            if tile < tiles - 1:
                ends[head, tile] = end
                if tile > 0:
                    middle = halves[head, tile, 0:1, :]
                    scale = middle * middle * (final(tile) == before(tile)).astype(F32)
                    eye = row_iota(shape) == lane_iota(shape)
                    carries[head, tile] = jnp.where(eye, scale, 0.0) - dot3(
                        end, keystate[head, rows, :]
                    )

    def store(index, tile, source, block):
        high, low = split(block)
        rows = pl.ds(tile * TILE, TILE)
        mats[index, rows, pl.ds(source * TILE, TILE)] = high
        mats[index, rows, pl.ds(rowtok + source * TILE, TILE)] = low

    def queries_part(members):
        where, grown, scores = [], [], []
        for index, head in enumerate(members):
            for tile in range(tiles):
                rows = pl.ds(tile * TILE, TILE)
                query = buf[2, rows, lanes(head)].astype(F32)
                query = (
                    query
                    * lax.rsqrt(jnp.sum(query * query, axis=-1, keepdims=True) + 1e-06)
                    * WIDTH ** (-0.5)
                )
                qg = query * growth[head, rows, :]
                score = dot3(qg, keyinv[head, rows, :], NT)
                scores.append(jnp.where(masks[tile, 1] > 0.0, score, 0.0))
                grown.append(qg)
                where.append((index, head, tile, rows))
        inner = [
            dot3(score, weights[head, rows, :])
            for (index, head, tile, rows), score in zip(where, scores)
        ]
        reads = []
        for (index, head, tile, rows), block, qg in zip(where, inner, grown):
            store(index, tile, tile, block)
            if tile > 0:
                first = (segcol[rows, :] == before(tile)).astype(F32) * halves[head, tile, 0:1, :]
                reads.append(qg * first - dot3(block, keystate[head, rows, :]))
            else:
                reads.append(None)
        for index, head in enumerate(members):
            for source in range(tiles - 1):
                state = ends[head, source]
                for tile in range(source + 1, tiles):
                    parts = split(state)
                    store(index, tile, source, dot3(reads[index * tiles + tile], parts))
                    if tile < tiles - 1:
                        state = dot3(carries[head, tile], parts)
        for index, head in enumerate(members):

            def move(step):
                rows = pl.ds(pl.multiple_of(step * TILE, TILE), TILE)
                placed[head, rows, :] = bdot(place[rows, :], mats[index]).astype(BF16)

            rows_of(slots // TILE, move)

    def values_part(head):
        value = buf[3, :, lanes(head)]
        value = jnp.concatenate([value, value], axis=0)
        gain = gain_ref[:, lanes(head)]
        for run in list(range(2, RUNS)) + [1, 0]:
            rows = pl.ds(run * capt, capt)
            result = bdot(placed[head, rows, :], value)
            norm = lax.rsqrt(jnp.mean(result * result, axis=-1, keepdims=True) + 1e-05)
            result = (result * norm * gain).astype(BF16)
            if run == 0:
                out_ref[rows, lanes(head)] = result
            else:
                stage[head, rows, :] = result
                outgoing(run, head).start()

    def of_value(matrix, value):
        high, low = split(matrix)
        return bdot(
            jnp.concatenate([high, low], axis=1), jnp.concatenate([value, value], axis=0)
        )

    def normed(result, gain):
        norm = lax.rsqrt(jnp.mean(result * result, axis=-1, keepdims=True) + 1e-05)
        return (result * norm * gain).astype(BF16)

    def tile_part(tile, items):
        rows = slice(tile * TILE, (tile + 1) * TILE)
        lower = (row_iota(shape) >= lane_iota(shape)).astype(F32).astype(BF16)
        seg = segcol[rows, :]
        kept, amats = [], []
        for load, place_of in items:
            values = betas[rows, :]
            beta = jnp.sum(
                jnp.where(lane_iota(values.shape) == place_of, values, 0.0), axis=1, keepdims=True
            )
            key = load(0).astype(F32)
            key = key * lax.rsqrt(jnp.sum(key * key, axis=-1, keepdims=True) + 1e-06)
            cumul = bdot(lower, load(1))
            mid = 0.5 * cumul[TILE - 1 :, :]
            grow = jnp.exp(cumul - mid)
            middle = jnp.exp(mid)
            kg, ki = key * grow, key * jnp.exp(mid - cumul)
            amat = jnp.where(masks[tile, 0] > 0.0, dot3(kg, ki, NT), 0.0)
            amats.append(amat * beta)
            query = load(2).astype(F32)
            query = (
                query
                * lax.rsqrt(jnp.sum(query * query, axis=-1, keepdims=True) + 1e-06)
                * WIDTH ** (-0.5)
            )
            qg = query * grow
            score = jnp.where(masks[tile, 1] > 0.0, dot3(qg, ki, NT), 0.0)
            kept.append((kg, ki, middle, qg, score))
        solved = [
            inv * brows[pl.ds(place_of, 1), :][:, rows]
            for (load, place_of), inv in zip(items, inverses(amats))
        ]
        inner = [dot3(score, w) for (kg, ki, middle, qg, score), w in zip(kept, solved)]
        if tile == 0:
            outer = [
                dot3(ki * ((seg == final(0)).astype(F32) * middle), w, TN)
                for (kg, ki, middle, qg, score), w in zip(kept, solved)
            ]
        else:
            outer = []
            for (kg, ki, middle, qg, score), block in zip(kept, inner):
                first = (seg == before(tile)).astype(F32) * middle
                outer.append(qg * first - dot3(block, kg * first))
        return inner, outer

    def put(head, both):
        full = bdot(place[...], both).astype(BF16)
        for run in list(range(2, RUNS)) + [1, 0]:
            rows = pl.ds(run * capt, capt)
            piece = full[run * capt : (run + 1) * capt]
            if run == 0:
                out_ref[rows, lanes(head)] = piece
            else:
                stage[head, rows, :] = piece
                outgoing(run, head).start()

    def role(low):
        home, other = kinds[low], kinds[not low]
        tile = 0 if low else 1
        area = slice(tile * TILE, (tile + 1) * TILE)

        def from_own(head):
            return (lambda w: buf[w, area, lanes(head)]), me * heads + head

        def from_other(head):
            return (lambda w: fbuf[w, :, lanes(head)]), mate * heads + head

        def settle(index):
            for step in cross + beside:
                parcel_to(low, step, index).wait_recv()

        def meet(part):
            for copy in states_over(part):
                copy.wait_recv()
            for slot in range(other) if part == 0 else range(other, home + other):
                result = (
                    dot3(reads[slot], coded[slot].astype(jnp.int32).astype(F32))
                    * sized[slot, 0:1, :]
                    + frees[slot]
                )
                if part == 0:
                    give[slot] = normed(result, fgain[:, lanes(slot)])
                else:
                    near[slot - other] = normed(result, gain_ref[:, lanes(slot - other)])
            if part == 0:
                half_over(low).start()

        def close():
            half_over(not low).wait_recv()
            for head in range(home):
                ordered = [near[head], got[head]] if low else [got[head], near[head]]
                put(head, jnp.concatenate(ordered, axis=0))

        def early(own, step):
            return early_own(low, step) if own else early_other(low, step)

        def phase(part):
            own = low == (part == 0)
            if own:
                items = [from_own(head) for head in range(home)]
            else:
                items = [from_other(head) for head in range(other)]
            shift = 0 if part == 0 else LOW_HOME
            for step in beside:
                early(own, step).wait_recv()
            inner, outer = tile_part(tile, items)
            values = [load(3) for load, place_of in items]
            if low:
                for slot, (block, value) in enumerate(zip(outer, values)):
                    state = of_value(block, value)
                    most = jnp.maximum(jnp.max(jnp.abs(state), axis=0, keepdims=True), 1e-30)
                    code = jnp.round(state * (32767.0 / most)).astype(jnp.int32)
                    codes[shift + slot] = code.astype(jnp.int16)
                    sizes[shift + slot] = jnp.broadcast_to(most * (1.0 / 32767.0), (8, WIDTH))
                for copy in states_over(part):
                    copy.start()
            for slot, (block, value) in enumerate(zip(inner, values)):
                result = of_value(block, value)
                if not low:
                    reads[shift + slot] = outer[slot]
                    frees[shift + slot] = result
                elif own:
                    near[slot] = normed(result, gain_ref[:, lanes(slot)])
                else:
                    give[slot] = normed(result, fgain[:, lanes(slot)])
            if low and not own:
                half_over(low).start()

        phase(0)
        for index in AFTER_ONE[low]:
            send_parcels(low, index)
        gain_over().wait_recv()
        phase(1)
        if not low:
            meet(0)
        for index in AFTER_TWO[low]:
            send_parcels(low, index)

        plan = homes(heads, home)
        for index, ((first, last), (begin, end)) in enumerate(plan):
            settle(index)
            for later in AFTER[low][index]:
                send_parcels(low, later)
            if first == 0:
                keys_part(list(range(begin, end)))
            elif first == 2:
                queries_part(list(range(begin, end)))
            else:
                for head in range(begin, end):
                    values_part(head)
            if index == CLOSE_AT[low]:
                if not low:
                    meet(1)
                close()
        for index in range(len(plan)):
            for step in beside:
                parcel_to(low, step, index).wait_send()
            for step in cross:
                parcel_to(not low, step, index).wait_send()
        for step in beside:
            early_own(low, step).wait_send()
            early_other(low, step).wait_send()
        if low:
            for copy in states_over(0) + states_over(1):
                copy.wait_send()
        gain_over().wait_send()
        half_over(low).wait_send()

    if shared:

        @pl.when(below)
        def _():
            role(True)

        @pl.when(jnp.logical_not(below))
        def _():
            role(False)

    else:
        group = mats.shape[0]
        for parcel, ((first, last), (low, high)) in enumerate(parcels):
            arrive(parcel)
            if parcel + AHEAD < len(parcels):
                for step in steps:
                    incoming(step, parcel + AHEAD).start()
            for begin in range(low, high, group):
                members = list(range(begin, min(begin + group, high)))
                if first == 0:
                    keys_part(members)
                if first <= 2 < last:
                    queries_part(members)
            if last == 4:
                for head in range(low, high):
                    values_part(head)

    for step in range(1, nz):
        incoming_beta(step).wait_send()
        for parcel in range(0 if shared else len(parcels)):
            incoming(step, parcel).wait_send()
    for head in range(heads):
        for run in range(1, RUNS):
            outgoing(run, head).wait()


def homes(heads, begin):
    early = heads - 1
    return [
        ((0, 2), (begin, heads)),
        ((2, 3), (begin, early)),
        ((3, 4), (begin, early)),
        ((2, 3), (early, heads)),
        ((3, 4), (early, heads)),
    ]


def parcels_of(heads):
    group = 2 if heads % 2 == 0 else 1
    pairs = [(low, low + group) for low in range(0, heads, group)]
    return (
        [((0, 2), pair) for pair in pairs]
        + [part for pair in pairs[:-1] for part in (((2, 3), pair), ((3, 4), pair))]
        + [((2, 3), pairs[-1])]
        + [((3, 4), (head, head + 1)) for head in range(*pairs[-1])]
    )


def solution(mesh):
    nz, nd = mesh.shape["head"], mesh.shape["doc"]

    def local(queries, keys, values, log_decay, beta_logit, block_owner, block_start, gain):
        tok, channels = queries.shape
        heads = channels // WIDTH // nz
        rowtok = tok * nz
        slots = 2 * rowtok
        tiles = rowtok // TILE
        shared = nz % 2 == 0 and tiles == 2 and tok * (nz // 2) == TILE and heads >= HIGH_HOME + 2
        group = heads - LOW_HOME if shared else 2 if heads % 2 == 0 else 1
        parcels = parcels_of(heads)
        most, both = max(LOW_HOME, HIGH_HOME), LOW_HOME + HIGH_HOME
        anywhere = pl.BlockSpec(memory_space=pl.ANY)
        dma = pltpu.SemaphoreType.DMA
        return pl.pallas_call(
            functools.partial(kernel, nz, nd, parcels, shared),
            out_shape=pltpu.VMEM((slots, heads * WIDTH), BF16),
            in_specs=[anywhere] * 8,
            out_specs=pl.BlockSpec(memory_space=pltpu.VMEM),
            scratch_shapes=[
                pltpu.VMEM((4, rowtok, heads * WIDTH), BF16),
                pltpu.VMEM((4, tok, channels), BF16),
                pltpu.VMEM((nz, beta_logit.shape[1], tok), BF16),
                pltpu.VMEM(block_owner.shape, jnp.int32),
                pltpu.VMEM(block_start.shape, jnp.int32),
                pltpu.VMEM((1, heads * WIDTH), F32),
                pltpu.VMEM((rowtok, beta_logit.shape[1]), F32),
                pltpu.VMEM((beta_logit.shape[1], rowtok), F32),
                pltpu.VMEM((slots, rowtok), BF16),
                pltpu.VMEM((heads, slots, WIDTH), BF16),
                pltpu.VMEM((rowtok, WIDTH), F32),
                pltpu.VMEM((tiles, 2, TILE, TILE), F32),
                pltpu.VMEM((heads, rowtok, WIDTH), F32),
                pltpu.VMEM((heads, rowtok, WIDTH), F32),
                pltpu.VMEM((heads, rowtok, WIDTH), F32),
                pltpu.VMEM((heads, tiles, 8, WIDTH), F32),
                pltpu.VMEM((heads, rowtok, WIDTH), F32),
                pltpu.VMEM((heads, tiles, WIDTH, WIDTH), F32),
                pltpu.VMEM((heads, tiles, WIDTH, WIDTH), F32),
                pltpu.VMEM((group, rowtok, 2 * rowtok), BF16),
                pltpu.VMEM((heads, slots, 2 * rowtok), BF16),
                dma((16,)),
                dma((nz, len(parcels))),
                dma((nz, len(parcels))),
                dma((nz,)),
                dma((nz,)),
                dma((RUNS, heads)),
                dma((RUNS, heads)),
                pltpu.SemaphoreType.REGULAR,
                pltpu.SemaphoreType.REGULAR,
            ]
            + [
                pltpu.VMEM((4, TILE, most * WIDTH), BF16),
                pltpu.VMEM((1, heads * WIDTH), F32),
                pltpu.VMEM((both, TILE, WIDTH), jnp.int16),
                pltpu.VMEM((both, TILE, WIDTH), jnp.int16),
                pltpu.VMEM((both, 8, WIDTH), F32),
                pltpu.VMEM((both, 8, WIDTH), F32),
                pltpu.VMEM((most, TILE, WIDTH), BF16),
                pltpu.VMEM((most, TILE, WIDTH), BF16),
                pltpu.VMEM((most, TILE, WIDTH), BF16),
                pltpu.VMEM((both, TILE, WIDTH), F32),
                pltpu.VMEM((both, TILE, WIDTH), F32),
                dma((nz, 2)),
                dma((nz, 2)),
                dma((6,)),
                dma((6,)),
            ]
            * shared,
            compiler_params=pltpu.CompilerParams(
                collective_id=0, has_side_effects=True, vmem_limit_bytes=60 * 1024 * 1024
            ),
            name="delta",
        )(
            queries, keys, values, log_decay, beta_logit.T, block_owner, block_start,
            gain.reshape(1, -1),
        )

    return jax.shard_map(
        local,
        mesh=mesh,
        in_specs=(P(("doc", "head"), None),) * 5 + (P(), P(), P("head")),
        out_specs=P("doc", "head"),
        check_vma=False,
    )
```
